128 devices in a mesh: orb: 64 (over y, x, z), pair: 2 (over core).
Axes of the slice: x: 4, y: 4, z: 4, core: 2. Of those that a mesh axis runs over, the one named last changes fastest.
Arguments:
- wavefunctions: float32 [128, 64, 4096], P(('orb', 'pair')), may hold values from -6 to 6
- potential: float32 [64, 4096], replicated, may hold values from -1.5 to 0.5
- line_runs: int32 [2, 4096], replicated, may hold values from 0 to 64, as said below
Outputs:
- gradient: float32 [128, 64, 4096], P(('orb', 'pair'))
- preconditioned: float32 [128, 64, 4096], P(('orb', 'pair'))
The draws below stay inside these ranges and needn't reach their ends.
Inputs may be any that keep to these rules, and one draw needn't show every extreme that they name: `line_runs`: exactly 3072 lines have start < end (runs of 1 to 32 points, start below 32); every other line has start = end = 0. The runs hold exactly 50688 grid points in all.
All inputs are finite; a program needn't handle non-finite values.
Results may differ from the reference program's by a relative error of at most 0.0001.
Values sent between devices are 32-bit elements; how exact they have to be, the bound alone decides.
A program may use at most 64 MiB of HBM per device.

```python
import math
import jax
import jax.numpy as jnp
import numpy as np
from jax import lax

GRID = 64
LIVE = 3072
CHEB = 6
ORBITALS = 128
CELLS = 262144


def draw_line_runs(key, part):
    lines_all = GRID * GRID
    score_key = jax.random.fold_in(key, 11)
    start_key = jax.random.fold_in(key, 12)
    length_key = jax.random.fold_in(key, 13)
    index = jnp.arange(lines_all, dtype=jnp.int32)
    first_pos = 2 * (index // GRID) - (GRID - 1)
    second_pos = 2 * (index % GRID) - (GRID - 1)
    radius = first_pos * first_pos + second_pos * second_pos
    noise = jax.random.randint(score_key, (lines_all,), 0, 2 * GRID * GRID, dtype=jnp.int32)
    score = (noise - radius // 2) * lines_all + index
    chosen = lax.top_k(score, LIVE)[1]
    live_flag = jnp.zeros((lines_all,), jnp.int32).at[chosen].set(1)
    line_rank = jnp.clip(jnp.cumsum(live_flag) - 1, 0, LIVE - 1).astype(jnp.int32)
    half_grid = GRID // 2
    pair_first = jax.random.randint(length_key, (LIVE // 2,), 1, half_grid + 1, dtype=jnp.int32)
    pair_value = jnp.take(pair_first, line_rank // 2)
    run_length = jnp.where(line_rank % 2 == 0, pair_value, half_grid + 1 - pair_value).astype(jnp.int32)
    run_start = jax.random.randint(start_key, (lines_all,), 0, half_grid, dtype=jnp.int32)
    lower = run_start * live_flag
    upper = (run_start + run_length) * live_flag
    return jnp.stack([lower, upper]).astype(jnp.int32)


def block_scale(stream_key, shape, shards, low, largest):
    loudness = 1.0
    for dim, shards_of in shards:
        draws = jax.random.uniform(jax.random.fold_in(jax.random.fold_in(stream_key, 6), dim), (shards_of,), jnp.float32, low / len(shards), largest / len(shards))
        loudness = loudness * jnp.repeat(jnp.exp(draws), shape[dim] // shards_of).reshape((-1,) + (1,) * (len(shape) - 1 - dim))
    return loudness


def bell_draw(stream_key, dims, width, most, shards=(), kind=jnp.bfloat16):
    factor_of = block_scale(stream_key, dims, shards, -0.22, 0.18) if shards else 1.0
    array = jax.random.normal(stream_key, dims, jnp.float32) * width * factor_of
    return jnp.minimum(jnp.maximum(array, -most), most).astype(kind)


def setup_inputs(seed: int = 0) -> dict:
    seeds = jax.random.split(jax.random.key(seed), 4)
    return {
        "wavefunctions": bell_draw(seeds[0], (ORBITALS, GRID, GRID * GRID), 1.0, 6.0, ((0, 128),), jnp.float32),
        "potential": jnp.clip(jax.random.uniform(seeds[1], (GRID, GRID * GRID), jnp.float32, -1.5, 0.5), -1.5, 0.5),
        "line_runs": draw_line_runs(jax.random.fold_in(seeds[3], 71), 0),
    }


KINETIC_SCALE = 0.125
SHIFT_VALUE = 0.25
HIGHEST_MODE = lax.Precision.HIGHEST


def kinetic_taps():
    radius = 14
    values = np.zeros(2 * radius + 1)
    factor = float(math.factorial(radius)) ** 2
    for offset in range(1, radius + 1):
        weight = 2.0 * (-1.0) ** (offset + 1) * factor / (offset * offset * float(math.factorial(radius - offset)) * float(math.factorial(radius + offset)))
        values[radius + offset] = weight
        values[radius - offset] = weight
    values[radius] = -2.0 * sum(1.0 / float(offset * offset) for offset in range(1, radius + 1))
    return values


def magic_taps():
    shifted = np.arange(-7, 9) - 0.25
    sinc_values = np.sin(np.pi * shifted) / (np.pi * shifted)
    values = sinc_values * (0.5 + 0.5 * np.cos(np.pi * shifted / 8.5))
    return values / values.sum()


def circulant(values, first, length):
    matrix = np.zeros((length, length))
    for target in range(length):
        for position in range(values.shape[0]):
            matrix[target, (target + first + position) % length] += values[position]
    return matrix


def kinetic_spectrum_top(length):
    taps = -KINETIC_SCALE * kinetic_taps()
    offsets = np.arange(-14, 15)
    modes = np.arange(length).reshape(length, 1)
    spectrum = np.cos(2.0 * np.pi * modes * offsets.reshape(1, -1) / length) @ taps
    return float(spectrum.max())


def filter_tables(length):
    kinetic = -KINETIC_SCALE * circulant(kinetic_taps(), -14, length)
    magic_matrix = circulant(magic_taps(), -7, length)
    low_end = SHIFT_VALUE
    high_end = SHIFT_VALUE + 3.0 * kinetic_spectrum_top(length)
    paired_kinetic = np.kron(np.eye(2), kinetic)
    paired_magic = np.kron(np.eye(2), magic_matrix)
    return (jnp.asarray(kinetic, jnp.float32), jnp.asarray(paired_kinetic, jnp.float32),
            jnp.asarray(magic_matrix, jnp.float32), jnp.asarray(paired_magic, jnp.float32),
            low_end, high_end)


def along_first(matrix, field_in):
    return jnp.einsum("nm,bmk->bnk", matrix, field_in, precision=HIGHEST_MODE)


def along_second(matrix, field_in):
    length = field_in.shape[1]
    shaped = field_in.reshape(field_in.shape[0], length, length, length)
    return jnp.einsum("nm,bxmz->bxnz", matrix, shaped, precision=HIGHEST_MODE).reshape(field_in.shape)


def along_third(paired, field_in):
    flat = field_in.reshape(-1, paired.shape[0])
    return jnp.dot(flat, paired.T, precision=HIGHEST_MODE, preferred_element_type=jnp.float32).reshape(field_in.shape)


def kinetic_apply(tables, field_in):
    return along_first(tables[0], field_in) + along_second(tables[0], field_in) + along_third(tables[1], field_in)


def hamiltonian(tables, potential, field_in):
    magic_matrix = tables[2]
    paired_magic = tables[3]
    real_space = along_third(paired_magic, along_second(magic_matrix, along_first(magic_matrix, field_in)))
    weighted = real_space * potential[None]
    returned = along_first(magic_matrix.T, along_second(magic_matrix.T, along_third(paired_magic.T, weighted)))
    return kinetic_apply(tables, field_in) + returned


def region_mask(line_runs):
    depths = jnp.arange(GRID, dtype=jnp.int32).reshape(1, 1, GRID)
    run_start = line_runs[0].reshape(GRID, GRID, 1)
    run_end = line_runs[1].reshape(GRID, GRID, 1)
    return ((depths >= run_start) & (depths < run_end)).astype(jnp.float32).reshape(GRID, GRID * GRID)


def chebyshev(tables, right_side):
    low_end = tables[4]
    high_end = tables[5]
    centre_value = 0.5 * (high_end + low_end)
    half_width = 0.5 * (high_end - low_end)
    ratio_base = centre_value / half_width
    rho_value = 1.0 / ratio_base
    solution = jnp.zeros_like(right_side)
    residual = right_side
    direction = right_side / centre_value
    for counter in range(CHEB):
        solution = solution + direction
        if counter + 1 < CHEB:
            residual = residual - (kinetic_apply(tables, direction) + SHIFT_VALUE * direction)
            rho_next = 1.0 / (2.0 * ratio_base - rho_value)
            direction = (rho_next * rho_value) * direction + (2.0 * rho_next / half_width) * residual
            rho_value = rho_next
    return solution


def reference(wavefunctions, potential, line_runs):
    tables = filter_tables(GRID)
    region = region_mask(line_runs)
    block_count = math.gcd(ORBITALS, 16)
    grouped = wavefunctions.reshape(ORBITALS // block_count, block_count, GRID, GRID * GRID)

    def apply_block(block_in):
        masked = block_in * region
        return masked, hamiltonian(tables, potential, masked)

    masked, applied = lax.map(apply_block, grouped)
    masked_flat = masked.reshape(ORBITALS, CELLS)
    applied_flat = applied.reshape(ORBITALS, CELLS)
    correlation = jnp.dot(masked_flat, applied_flat.T, precision=HIGHEST_MODE, preferred_element_type=jnp.float32) / CELLS
    projected = lax.dot_general(correlation, masked_flat, (((0,), (0,)), ((), ())), precision=HIGHEST_MODE, preferred_element_type=jnp.float32)
    gradient = (applied_flat - projected).reshape(ORBITALS, GRID, GRID * GRID) * region

    def precondition(block_in):
        return chebyshev(tables, block_in) * region

    preconditioned = lax.map(precondition, gradient.reshape(grouped.shape)).reshape(gradient.shape)
    return gradient, preconditioned
```

```python
import math

import jax
import jax.numpy as jnp
import numpy as np
from jax import lax
from jax.experimental import pallas as pl
from jax.experimental.pallas import tpu as pltpu
from jax.sharding import PartitionSpec as P

GRID = 64
CHEB = 6


KINETIC_SCALE = 0.125
SHIFT_VALUE = 0.25
HIGHEST_MODE = lax.Precision.HIGHEST


def kinetic_taps():
    radius = 14
    values = np.zeros(2 * radius + 1)
    factor = float(math.factorial(radius)) ** 2
    for offset in range(1, radius + 1):
        weight = (
            2.0
            * (-1.0) ** (offset + 1)
            * factor
            / (
                offset
                * offset
                * float(math.factorial(radius - offset))
                * float(math.factorial(radius + offset))
            )
        )
        values[radius + offset] = weight
        values[radius - offset] = weight
    values[radius] = -2.0 * sum((1.0 / float(offset * offset) for offset in range(1, radius + 1)))
    return values


def magic_taps():
    shifted = np.arange(-7, 9) - 0.25
    sinc_values = np.sin(np.pi * shifted) / (np.pi * shifted)
    values = sinc_values * (0.5 + 0.5 * np.cos(np.pi * shifted / 8.5))
    return values / values.sum()


def circulant(values, first, length):
    matrix = np.zeros((length, length))
    for target in range(length):
        for position in range(values.shape[0]):
            matrix[target, (target + first + position) % length] += values[position]
    return matrix


def kinetic_spectrum_top(length):
    taps = -KINETIC_SCALE * kinetic_taps()
    offsets = np.arange(-14, 15)
    modes = np.arange(length).reshape(length, 1)
    spectrum = np.cos(2.0 * np.pi * modes * offsets.reshape(1, -1) / length) @ taps
    return float(spectrum.max())


def filter_tables(length):
    kinetic = -KINETIC_SCALE * circulant(kinetic_taps(), -14, length)
    magic_matrix = circulant(magic_taps(), -7, length)
    low_end = SHIFT_VALUE
    high_end = SHIFT_VALUE + 3.0 * kinetic_spectrum_top(length)
    paired_kinetic = np.kron(np.eye(2), kinetic)
    paired_magic = np.kron(np.eye(2), magic_matrix)
    return (
        jnp.asarray(kinetic, jnp.float32),
        jnp.asarray(paired_kinetic, jnp.float32),
        jnp.asarray(magic_matrix, jnp.float32),
        jnp.asarray(paired_magic, jnp.float32),
        low_end,
        high_end,
    )


def along_first(matrix, field_in):
    return jnp.einsum("nm,bmk->bnk", matrix, field_in, precision=HIGHEST_MODE)


def along_second(matrix, field_in):
    length = field_in.shape[1]
    shaped = field_in.reshape(field_in.shape[0], length, length, length)
    return jnp.einsum("nm,bxmz->bxnz", matrix, shaped, precision=HIGHEST_MODE).reshape(
        field_in.shape
    )


def along_third(paired, field_in):
    flat = field_in.reshape(-1, paired.shape[0])
    return jnp.dot(
        flat, paired.T, precision=HIGHEST_MODE, preferred_element_type=jnp.float32
    ).reshape(field_in.shape)


def kinetic_apply(tables, field_in):
    return (
        along_first(tables[0], field_in)
        + along_second(tables[0], field_in)
        + along_third(tables[1], field_in)
    )


def hamiltonian(tables, potential, field_in):
    magic_matrix = tables[2]
    paired_magic = tables[3]
    real_space = along_third(
        paired_magic, along_second(magic_matrix, along_first(magic_matrix, field_in))
    )
    weighted = real_space * potential[None]
    returned = along_first(
        magic_matrix.T, along_second(magic_matrix.T, along_third(paired_magic.T, weighted))
    )
    return kinetic_apply(tables, field_in) + returned


def region_mask(line_runs):
    depths = jnp.arange(GRID, dtype=jnp.int32).reshape(1, 1, GRID)
    run_start = line_runs[0].reshape(GRID, GRID, 1)
    run_end = line_runs[1].reshape(GRID, GRID, 1)
    return (
        ((depths >= run_start) & (depths < run_end)).astype(jnp.float32).reshape(GRID, GRID * GRID)
    )


def chebyshev(tables, right_side):
    low_end = tables[4]
    high_end = tables[5]
    centre_value = 0.5 * (high_end + low_end)
    half_width = 0.5 * (high_end - low_end)
    ratio_base = centre_value / half_width
    rho_value = 1.0 / ratio_base
    solution = jnp.zeros_like(right_side)
    residual = right_side
    direction = right_side / centre_value
    for counter in range(CHEB):
        solution = solution + direction
        if counter + 1 < CHEB:
            residual = residual - (kinetic_apply(tables, direction) + SHIFT_VALUE * direction)
            rho_next = 1.0 / (2.0 * ratio_base - rho_value)
            direction = rho_next * rho_value * direction + 2.0 * rho_next / half_width * residual
            rho_value = rho_next
    return solution


DEVICES = 128
MESH_IDS = pl.DeviceIdType.MESH


def split_pair(value):
    high = value.astype(jnp.bfloat16)
    low = (value - high.astype(jnp.float32)).astype(jnp.bfloat16)
    return high, low


def tile_of(index):
    return pl.ds(pl.multiple_of(index * 8, 8), 8)


def peer_id(index):
    return (index // 2, lax.rem(index, 2))


def exchange_kernel(
    masked_send, applied_send, gradient_out,
    masked_recv, applied_recv, back_send, partial, gathered, row, matrix,
    send_sems, recv_sems,
):
    me = lax.axis_index("orb") * 2 + lax.axis_index("pair")
    barrier = pltpu.get_barrier_semaphore()

    def peer_at(step):
        return lax.rem(me + step, DEVICES)

    def greet(step, carry):
        pl.semaphore_signal(barrier, inc=1, device_id=peer_id(peer_at(step)), device_id_type=MESH_IDS)
        return carry

    lax.fori_loop(1, DEVICES, greet, 0)
    pl.semaphore_wait(barrier, DEVICES - 1)

    def scatter(source, target, phase, source_at, target_at):
        def send(step, carry):
            peer = peer_at(step)
            pltpu.make_async_remote_copy(
                src_ref=source.at[source_at(peer)],
                dst_ref=target.at[target_at(me)],
                send_sem=send_sems.at[phase],
                recv_sem=recv_sems.at[phase],
                device_id=peer_id(peer),
                device_id_type=MESH_IDS,
            ).start()
            return carry

        lax.fori_loop(1, DEVICES, send, 0)

    def drain(buffer, sem):
        whole = buffer.at[pl.ds(0, buffer.shape[0] * (DEVICES - 1) // DEVICES)]
        pltpu.make_async_copy(whole, whole, sem).wait()

    def row_of(index):
        return pl.ds(index, 1)

    scatter(masked_send, masked_recv, 0, tile_of, tile_of)
    scatter(applied_send, applied_recv, 1, tile_of, tile_of)
    masked_recv[tile_of(me), :] = masked_send[tile_of(me), :]
    applied_recv[tile_of(me), :] = applied_send[tile_of(me), :]
    drain(masked_recv, recv_sems.at[0])
    drain(applied_recv, recv_sems.at[1])

    total = jnp.zeros((DEVICES, DEVICES), jnp.float32)
    for sub in range(8):
        masked_high, masked_low = split_pair(masked_recv[pl.ds(sub, DEVICES, stride=8), :])
        applied_high, applied_low = split_pair(applied_recv[pl.ds(sub, DEVICES, stride=8), :])
        for left, right in ((applied_high, masked_high), (applied_high, masked_low), (applied_low, masked_high)):
            total = total + lax.dot_general(
                left, right, (((1,), (1,)), ((), ())), preferred_element_type=jnp.float32
            )
    partial[:, 0, :] = total
    scatter(partial, gathered, 2, row_of, row_of)
    gathered[row_of(me)] = partial[row_of(me)]
    drain(gathered, recv_sems.at[2])
    row[...] = jnp.sum(gathered[...], axis=0, keepdims=True) * (1.0 / (GRID * GRID * GRID))
    scatter(row, matrix, 3, lambda peer: pl.ds(0, 1), row_of)
    matrix[row_of(me)] = row[...]
    drain(matrix, recv_sems.at[3])
    matrix_high, matrix_low = split_pair(matrix[:, 0, :])
    for sub in range(8):
        rows = pl.ds(sub, DEVICES, stride=8)
        masked_high, masked_low = split_pair(masked_recv[rows, :])
        projected = jnp.dot(matrix_high, masked_high, preferred_element_type=jnp.float32)
        projected = projected + jnp.dot(matrix_high, masked_low, preferred_element_type=jnp.float32)
        projected = projected + jnp.dot(matrix_low, masked_high, preferred_element_type=jnp.float32)
        back_send[rows, :] = applied_recv[rows, :] - projected
    scatter(back_send, gradient_out, 4, tile_of, tile_of)
    gradient_out[tile_of(me), :] = back_send[tile_of(me), :]
    drain(gradient_out, recv_sems.at[4])
    drain(masked_send, send_sems.at[0])
    drain(applied_send, send_sems.at[1])
    drain(partial, send_sems.at[2])
    drain(matrix, send_sems.at[3])
    drain(back_send, send_sems.at[4])


def exchange(masked_tiles, applied_tiles):
    tiles = (8 * DEVICES, 128)
    return pl.pallas_call(
        exchange_kernel,
        out_shape=jax.ShapeDtypeStruct(tiles, jnp.float32),
        in_specs=[pl.BlockSpec(memory_space=pltpu.VMEM)] * 2,
        out_specs=pl.BlockSpec(memory_space=pltpu.VMEM),
        scratch_shapes=[
            pltpu.VMEM(tiles, jnp.float32),
            pltpu.VMEM(tiles, jnp.float32),
            pltpu.VMEM(tiles, jnp.float32),
            pltpu.VMEM((DEVICES, 1, 128), jnp.float32),
            pltpu.VMEM((DEVICES, 1, 128), jnp.float32),
            pltpu.VMEM((1, 1, 128), jnp.float32),
            pltpu.VMEM((DEVICES, 1, 128), jnp.float32),
            pltpu.SemaphoreType.DMA((5,)),
            pltpu.SemaphoreType.DMA((5,)),
        ],
        compiler_params=pltpu.CompilerParams(collective_id=0, has_side_effects=True),
        name="exchange",
    )(masked_tiles, applied_tiles)


def folded(field_in):
    split = field_in.reshape(GRID, GRID, 2, 32)
    return (split[:, :, 0] + split[:, :, 1]).reshape(1024, 128)


def unfolded(tiles, region):
    split = jnp.broadcast_to(tiles.reshape(GRID, GRID, 1, 32), (GRID, GRID, 2, 32))
    return split.reshape(1, GRID, GRID * GRID) * region


def on_device(wavefunctions, potential, line_runs):
    tables = filter_tables(GRID)
    region = region_mask(line_runs)
    masked = wavefunctions * region
    applied = hamiltonian(tables, potential, masked)
    tiles = exchange(folded(masked[0]), folded(applied[0] * region))
    gradient = unfolded(tiles, region)
    preconditioned = chebyshev(tables, gradient) * region
    return (gradient, preconditioned)


def solution(mesh):
    return jax.shard_map(
        on_device,
        mesh=mesh,
        in_specs=(P(("orb", "pair"), None, None), P(), P()),
        out_specs=(P(("orb", "pair"), None, None), P(("orb", "pair"), None, None)),
        check_vma=False,
    )
```

```python
import math

import jax
import jax.numpy as jnp
import numpy as np
from jax import lax
from jax.experimental import pallas as pl
from jax.experimental.pallas import tpu as pltpu
from jax.sharding import PartitionSpec as P

GRID = 64
CHEB = 6
CELLS = GRID * GRID * GRID
PLANES = GRID // 2
DEVICES = 128
MESH_IDS = pl.DeviceIdType.MESH
KINETIC_SCALE = 0.125
SHIFT_VALUE = 0.25
VMEM_LIMIT = 56 * 1024 * 1024
BF16 = jnp.bfloat16
F32 = jnp.float32


def kinetic_taps():
    radius = 14
    values = np.zeros(2 * radius + 1)
    factor = float(math.factorial(radius)) ** 2
    for offset in range(1, radius + 1):
        weight = (
            2.0
            * (-1.0) ** (offset + 1)
            * factor
            / (
                offset
                * offset
                * float(math.factorial(radius - offset))
                * float(math.factorial(radius + offset))
            )
        )
        values[radius + offset] = weight
        values[radius - offset] = weight
    values[radius] = -2.0 * sum((1.0 / float(offset * offset) for offset in range(1, radius + 1)))
    return values


def magic_taps():
    shifted = np.arange(-7, 9) - 0.25
    sinc_values = np.sin(np.pi * shifted) / (np.pi * shifted)
    values = sinc_values * (0.5 + 0.5 * np.cos(np.pi * shifted / 8.5))
    return values / values.sum()


def circulant(values, first, length):
    matrix = np.zeros((length, length))
    for target in range(length):
        for position in range(values.shape[0]):
            matrix[target, (target + first + position) % length] += values[position]
    return matrix


def kinetic_spectrum():
    taps = -KINETIC_SCALE * kinetic_taps()
    offsets = np.arange(-14, 15)
    modes = np.arange(GRID).reshape(GRID, 1)
    return np.cos(2.0 * np.pi * modes * offsets.reshape(1, -1) / GRID) @ taps


def hartley():
    angle = 2.0 * np.pi * np.outer(np.arange(GRID), np.arange(GRID)) / GRID
    return (np.cos(angle) + np.sin(angle)) / np.sqrt(GRID)


def chebyshev_symbol():
    line = kinetic_spectrum()
    low_end = SHIFT_VALUE
    high_end = SHIFT_VALUE + 3.0 * float(line.max())
    centre_value = 0.5 * (high_end + low_end)
    half_width = 0.5 * (high_end - low_end)
    ratio_base = centre_value / half_width
    rho_value = 1.0 / ratio_base
    operator = line[:, None, None] + line[None, :, None] + line[None, None, :] + SHIFT_VALUE
    solution_value = np.zeros_like(operator)
    residual = np.ones_like(operator)
    direction = residual / centre_value
    for counter in range(CHEB):
        solution_value = solution_value + direction
        if counter + 1 < CHEB:
            residual = residual - operator * direction
            rho_next = 1.0 / (2.0 * ratio_base - rho_value)
            direction = rho_next * rho_value * direction + 2.0 * rho_next / half_width * residual
            rho_value = rho_next
    return solution_value.reshape(GRID * PLANES, 128).astype(np.float32)


def split_table(matrix):
    high = np.asarray(matrix, np.float32).astype(jnp.bfloat16)
    low = (np.asarray(matrix, np.float64) - high.astype(np.float64)).astype(np.float32).astype(jnp.bfloat16)
    return high, low


def rows_table(matrix):
    high, low = split_table(matrix)
    return np.concatenate([high, high, low], axis=1)


def lanes_table(*matrices):
    wide = np.concatenate([np.kron(np.eye(2), matrix.T) for matrix in matrices], axis=1)
    high, low = split_table(wide)
    return np.concatenate([high, high, low], axis=0)


def planes_table(matrix):
    even = np.concatenate([matrix[0::2, 0::2], matrix[0::2, 1::2]], axis=1)
    odd = np.concatenate([matrix[1::2, 1::2], matrix[1::2, 0::2]], axis=1)
    return rows_table(np.concatenate([even, odd], axis=0))


def split_pair(value):
    high = value.astype(BF16)
    low = (value - high.astype(F32)).astype(BF16)
    return high, low


def dot32(left, right):
    return jnp.dot(left, right, preferred_element_type=F32)


def along_rows(table, value):
    high, low = split_pair(value)
    return dot32(table, jnp.concatenate([high, low, high], axis=0))


def along_lanes(table, value):
    high, low = split_pair(value)
    return dot32(jnp.concatenate([high, low], axis=1), table[:256]) + dot32(high, table[256:])


def lane_index(shape):
    return lax.broadcasted_iota(jnp.int32, shape, 1)


def plane_stack(value):
    swapped = jnp.concatenate(
        [pltpu.roll(value[:, :128], 64, 1), pltpu.roll(value[:, 128:], 64, 1)], axis=1
    )
    high, low = split_pair(jnp.concatenate([value, swapped], axis=0))
    return jnp.concatenate([high, low, high], axis=0)


def plane_pick(product):
    half = lane_index((PLANES, 256)) % 128 < 64
    return jnp.where(half, product[:PLANES], product[PLANES:])


def two_planes(ref, first):
    return jnp.concatenate(
        [ref[pl.ds(first, PLANES, stride=GRID), :], ref[pl.ds(first + 1, PLANES, stride=GRID), :]],
        axis=1,
    )


def put_two_planes(ref, first, value):
    ref[pl.ds(first, PLANES, stride=GRID), :] = value[:, :128]
    ref[pl.ds(first + 1, PLANES, stride=GRID), :] = value[:, 128:]


def block_of(plane):
    return pl.ds(pl.multiple_of(plane * GRID, GRID), GRID)


def run_bounds(runs):
    row = lax.broadcasted_iota(jnp.int32, (GRID, PLANES), 0)
    column = lax.broadcasted_iota(jnp.int32, (GRID, PLANES), 1)
    repeat = (row // 2 == column).astype(F32).astype(BF16)
    own = lax.broadcasted_iota(jnp.int32, (GRID, 128), 0) % 2 == lane_index((GRID, 128)) // 64
    bounds = []
    for bound in range(2):
        lines = runs[bound : bound + 1, :].reshape(PLANES, 128).astype(F32).astype(BF16)
        bounds.append(jnp.where(own, dot32(repeat, lines), 0.0))
    return jnp.concatenate(bounds, axis=0).astype(BF16)


def region_pair(bounds, pair):
    lane = lane_index((128, 256))
    line = lax.broadcasted_iota(jnp.int32, (128, 256), 0) % GRID
    pick = (line == lane // 64 + 4 * pair).astype(F32).astype(BF16)
    spread = dot32(bounds, pick)
    depth = (lane_index((GRID, 256)) % GRID).astype(F32)
    return ((depth >= spread[:GRID]) & (depth < spread[GRID:])).astype(F32)


def fold_pair(value):
    first, second = value[:, :128], value[:, 128:]
    lower = (lane_index((GRID, 128)) // 32) % 2 == 0
    return jnp.where(lower, first + pltpu.roll(first, 96, 1), second + pltpu.roll(second, 32, 1))


def unfold_pair(tile):
    lower = (lane_index((GRID, 128)) // 32) % 2 == 0
    first = jnp.where(lower, tile, pltpu.roll(tile, 32, 1))
    second = jnp.where(lower, pltpu.roll(tile, 96, 1), tile)
    return jnp.concatenate([first, second], axis=1)


def load_planes(hbm, vmem, sem):
    for plane in range(PLANES):
        pltpu.make_async_copy(
            hbm.at[:, pl.ds(plane * 128, 128)], vmem.at[pl.ds(plane * GRID, GRID), :], sem
        ).start()


def wait_planes(vmem, sem):
    pltpu.make_async_copy(vmem, vmem, sem).wait()


def both_planes(ref, pair):
    return jnp.concatenate([ref[block_of(2 * pair), :], ref[block_of(2 * pair + 1), :]], axis=1)


def put_both_planes(ref, pair, value):
    ref[block_of(2 * pair), :] = value[:, :128]
    ref[block_of(2 * pair + 1), :] = value[:, 128:]


def lanes_pair(table, value):
    stacked = along_lanes(table, jnp.concatenate([value[:, :128], value[:, 128:]], axis=0))
    return stacked[:GRID], stacked[GRID:]


HALF_LOOP = 16


def hamiltonian_head(masked, kinetic, forward, tables, pair, value):
    lanes_kf, rows_k, rows_f = tables
    first, second = lanes_pair(lanes_kf[...], value)
    put_both_planes(masked, pair, value)
    along = jnp.concatenate([first[:, :128], second[:, :128]], axis=1) + along_rows(rows_k[...], value)
    put_both_planes(kinetic, pair, along)
    magic = jnp.concatenate([first[:, 128:], second[:, 128:]], axis=1)
    put_both_planes(forward, pair, along_rows(rows_f[...], magic))


def hamiltonian_middle(masked, kinetic, forward, potential, tables, step):
    planes_k, planes_f, planes_b = tables
    first = 2 * step
    real = plane_pick(dot32(planes_f[...], plane_stack(two_planes(forward, first))))
    weighted = real * two_planes(potential, first)
    put_two_planes(forward, first, plane_pick(dot32(planes_b[...], plane_stack(weighted))))
    along = plane_pick(dot32(planes_k[...], plane_stack(two_planes(masked, first))))
    put_two_planes(kinetic, first, two_planes(kinetic, first) + along)


def hamiltonian_tail(kinetic, forward, tables, pair):
    rows_b, lanes_b = tables
    first, second = lanes_pair(lanes_b[...], along_rows(rows_b[...], both_planes(forward, pair)))
    return both_planes(kinetic, pair) + jnp.concatenate([first, second], axis=1)


def loop(count, body, unroll=1):
    def step(index, carry):
        body(index)
        return carry

    lax.fori_loop(0, count, step, 0, unroll=unroll)


def precondition_kernel(
    tiles, runs, lanes_q, rows_q, planes_q, symbol_hbm, gradient_out, preconditioned_out,
    region, gradient, work, symbol, sems,
):
    fetch = pltpu.make_async_copy(symbol_hbm, symbol, sems.at[0])
    fetch.start()
    bounds = run_bounds(runs[...])

    def put(buffer, target, plane, sem):
        return pltpu.make_async_copy(
            buffer.at[block_of(plane), :],
            target.at[0, :, pl.ds(pl.multiple_of(plane * 128, 128), 128)],
            sem,
        )

    def head(pair):
        mask = region_pair(bounds, pair)
        put_both_planes(region, pair, mask)
        value = unfold_pair(tiles[block_of(pair), :]) * mask
        put_both_planes(gradient, pair, value)
        put(gradient, gradient_out, 2 * pair, sems.at[1]).start()
        put(gradient, gradient_out, 2 * pair + 1, sems.at[1]).start()
        first, second = lanes_pair(lanes_q[...], value)
        put_both_planes(work, pair, along_rows(rows_q[...], jnp.concatenate([first, second], axis=1)))

    loop(PLANES // 2, head, HEAD_UNROLL)
    fetch.wait()

    def middle(step):
        first = 2 * step
        modes = plane_pick(dot32(planes_q[...], plane_stack(two_planes(work, first))))
        factor = jnp.concatenate([symbol[pl.ds(pl.multiple_of(first * PLANES, 64), PLANES), :],
                                  symbol[pl.ds(pl.multiple_of(first * PLANES, 64) + PLANES, PLANES), :]], axis=1)
        put_two_planes(work, first, plane_pick(dot32(planes_q[...], plane_stack(modes * factor))))

    loop(GRID // 2, middle, MIDDLE_UNROLL)
    wait_planes(gradient, sems.at[1])

    def tail(pair):
        first, second = lanes_pair(lanes_q[...], along_rows(rows_q[...], both_planes(work, pair)))
        value = jnp.concatenate([first, second], axis=1) * both_planes(region, pair)
        put_both_planes(work, pair, value)
        put(work, preconditioned_out, 2 * pair, sems.at[2]).start()
        put(work, preconditioned_out, 2 * pair + 1, sems.at[2]).start()

    loop(PLANES // 2, tail, HEAD_UNROLL)
    wait_planes(work, sems.at[2])


HEAD_UNROLL = 4
MIDDLE_UNROLL = 4


def in_vmem(count):
    return [pl.BlockSpec(memory_space=pltpu.VMEM)] * count


def precondition(tiles, line_runs):
    modes = hartley()
    field = pltpu.VMEM((GRID * PLANES, 128), F32)
    shape = jax.ShapeDtypeStruct((1, GRID, GRID * GRID), F32)
    return pl.pallas_call(
        precondition_kernel,
        out_shape=(shape, shape),
        in_specs=in_vmem(5) + [pl.BlockSpec(memory_space=pl.ANY)],
        out_specs=[pl.BlockSpec(memory_space=pl.ANY)] * 2,
        scratch_shapes=[field, field, field, field, pltpu.SemaphoreType.DMA((3,))],
        compiler_params=pltpu.CompilerParams(vmem_limit_bytes=VMEM_LIMIT),
        name="precondition",
    )(
        tiles,
        line_runs,
        jnp.asarray(lanes_table(modes)),
        jnp.asarray(rows_table(modes)),
        jnp.asarray(planes_table(modes)),
        jnp.asarray(chebyshev_symbol()),
    )


def apply_kernel(
    wave, potential_hbm, runs, lanes_kf, rows_k, rows_f, planes_k, planes_f, planes_b, rows_b, lanes_b,
    masked_tiles, applied_tiles,
    region, masked, kinetic, forward, potential, sems,
):
    load_planes(wave.at[0], masked, sems.at[0])
    load_planes(potential_hbm, potential, sems.at[1])
    bounds = run_bounds(runs[...])
    wait_planes(masked, sems.at[0])

    def head(pair):
        mask = region_pair(bounds, pair)
        put_both_planes(region, pair, mask)
        value = both_planes(masked, pair) * mask
        masked_tiles[block_of(pair), :] = fold_pair(value)
        hamiltonian_head(masked, kinetic, forward, (lanes_kf, rows_k, rows_f), pair, value)

    loop(PLANES // 2, head, HEAD_UNROLL)
    wait_planes(potential, sems.at[1])
    loop(
        GRID // 2,
        lambda step: hamiltonian_middle(
            masked, kinetic, forward, potential, (planes_k, planes_f, planes_b), step
        ),
        MIDDLE_UNROLL,
    )

    def tail(pair):
        value = hamiltonian_tail(kinetic, forward, (rows_b, lanes_b), pair) * both_planes(region, pair)
        applied_tiles[block_of(pair), :] = fold_pair(value)

    loop(PLANES // 2, tail, HEAD_UNROLL)


def hamiltonian_tables():
    kinetic = -KINETIC_SCALE * circulant(kinetic_taps(), -14, GRID)
    magic = circulant(magic_taps(), -7, GRID)
    tables = (
        lanes_table(kinetic, magic),
        rows_table(kinetic),
        rows_table(magic),
        planes_table(kinetic),
        planes_table(magic),
        planes_table(magic.T),
        rows_table(magic.T),
        lanes_table(magic.T),
    )
    return [jnp.asarray(table) for table in tables]


def apply_fields(wavefunctions, potential, line_runs):
    field = pltpu.VMEM((GRID * PLANES, 128), F32)
    tiles = jax.ShapeDtypeStruct((8 * DEVICES, 128), F32)
    anywhere = [pl.BlockSpec(memory_space=pl.ANY)]
    return pl.pallas_call(
        apply_kernel,
        out_shape=(tiles, tiles),
        in_specs=anywhere * 2 + in_vmem(9),
        out_specs=in_vmem(2),
        scratch_shapes=[field, field, field, field, field, pltpu.SemaphoreType.DMA((2,))],
        compiler_params=pltpu.CompilerParams(vmem_limit_bytes=VMEM_LIMIT),
        name="apply",
    )(wavefunctions, potential, line_runs, *hamiltonian_tables())


def tile_of(index):
    return pl.ds(pl.multiple_of(index * 8, 8), 8)


def peer_id(index):
    return (index // 2, lax.rem(index, 2))


def exchange_kernel(
    masked_send, applied_send, gradient_out,
    masked_recv, applied_recv, back_send, partial, gathered, row, matrix,
    send_sems, recv_sems,
):
    me = lax.axis_index("orb") * 2 + lax.axis_index("pair")
    barrier = pltpu.get_barrier_semaphore()

    def peer_at(step):
        return lax.rem(me + step, DEVICES)

    def greet(step, carry):
        pl.semaphore_signal(barrier, inc=1, device_id=peer_id(peer_at(step)), device_id_type=MESH_IDS)
        return carry

    lax.fori_loop(1, DEVICES, greet, 0)
    pl.semaphore_wait(barrier, DEVICES - 1)

    def scatter(source, target, phase, source_at, target_at):
        def send(step, carry):
            peer = peer_at(step)
            pltpu.make_async_remote_copy(
                src_ref=source.at[source_at(peer)],
                dst_ref=target.at[target_at(me)],
                send_sem=send_sems.at[phase],
                recv_sem=recv_sems.at[phase],
                device_id=peer_id(peer),
                device_id_type=MESH_IDS,
            ).start()
            return carry

        lax.fori_loop(1, DEVICES, send, 0)

    def drain(buffer, sem):
        whole = buffer.at[pl.ds(0, buffer.shape[0] * (DEVICES - 1) // DEVICES)]
        pltpu.make_async_copy(whole, whole, sem).wait()

    def row_of(index):
        return pl.ds(index, 1)

    scatter(masked_send, masked_recv, 0, tile_of, tile_of)
    scatter(applied_send, applied_recv, 1, tile_of, tile_of)
    masked_recv[tile_of(me), :] = masked_send[tile_of(me), :]
    applied_recv[tile_of(me), :] = applied_send[tile_of(me), :]
    drain(masked_recv, recv_sems.at[0])
    drain(applied_recv, recv_sems.at[1])

    total = jnp.zeros((DEVICES, DEVICES), jnp.float32)
    for sub in range(8):
        masked_high, masked_low = split_pair(masked_recv[pl.ds(sub, DEVICES, stride=8), :])
        applied_high, applied_low = split_pair(applied_recv[pl.ds(sub, DEVICES, stride=8), :])
        for left, right in ((applied_high, masked_high), (applied_high, masked_low), (applied_low, masked_high)):
            total = total + lax.dot_general(
                left, right, (((1,), (1,)), ((), ())), preferred_element_type=jnp.float32
            )
    partial[:, 0, :] = total
    scatter(partial, gathered, 2, row_of, row_of)
    gathered[row_of(me)] = partial[row_of(me)]
    drain(gathered, recv_sems.at[2])
    row[...] = jnp.sum(gathered[...], axis=0, keepdims=True) * (1.0 / (GRID * GRID * GRID))
    scatter(row, matrix, 3, lambda peer: pl.ds(0, 1), row_of)
    matrix[row_of(me)] = row[...]
    drain(matrix, recv_sems.at[3])
    matrix_high, matrix_low = split_pair(matrix[:, 0, :])
    for sub in range(8):
        rows = pl.ds(sub, DEVICES, stride=8)
        masked_high, masked_low = split_pair(masked_recv[rows, :])
        projected = jnp.dot(matrix_high, masked_high, preferred_element_type=jnp.float32)
        projected = projected + jnp.dot(matrix_high, masked_low, preferred_element_type=jnp.float32)
        projected = projected + jnp.dot(matrix_low, masked_high, preferred_element_type=jnp.float32)
        back_send[rows, :] = applied_recv[rows, :] - projected
    scatter(back_send, gradient_out, 4, tile_of, tile_of)
    gradient_out[tile_of(me), :] = back_send[tile_of(me), :]
    drain(gradient_out, recv_sems.at[4])
    drain(masked_send, send_sems.at[0])
    drain(applied_send, send_sems.at[1])
    drain(partial, send_sems.at[2])
    drain(matrix, send_sems.at[3])
    drain(back_send, send_sems.at[4])


def exchange(masked_tiles, applied_tiles):
    tiles = (8 * DEVICES, 128)
    return pl.pallas_call(
        exchange_kernel,
        out_shape=jax.ShapeDtypeStruct(tiles, jnp.float32),
        in_specs=[pl.BlockSpec(memory_space=pltpu.VMEM)] * 2,
        out_specs=pl.BlockSpec(memory_space=pltpu.VMEM),
        scratch_shapes=[
            pltpu.VMEM(tiles, jnp.float32),
            pltpu.VMEM(tiles, jnp.float32),
            pltpu.VMEM(tiles, jnp.float32),
            pltpu.VMEM((DEVICES, 1, 128), jnp.float32),
            pltpu.VMEM((DEVICES, 1, 128), jnp.float32),
            pltpu.VMEM((1, 1, 128), jnp.float32),
            pltpu.VMEM((DEVICES, 1, 128), jnp.float32),
            pltpu.SemaphoreType.DMA((5,)),
            pltpu.SemaphoreType.DMA((5,)),
        ],
        compiler_params=pltpu.CompilerParams(collective_id=0, has_side_effects=True),
        name="exchange",
    )(masked_tiles, applied_tiles)


def on_device(wavefunctions, potential, line_runs):
    masked_tiles, applied_tiles = apply_fields(wavefunctions, potential, line_runs)
    tiles = exchange(masked_tiles, applied_tiles)
    return precondition(tiles, line_runs)


def solution(mesh):
    return jax.shard_map(
        on_device,
        mesh=mesh,
        in_specs=(P(("orb", "pair"), None, None), P(), P()),
        out_specs=(P(("orb", "pair"), None, None), P(("orb", "pair"), None, None)),
        check_vma=False,
    )
```

```python
import math

import jax
import jax.numpy as jnp
import numpy as np
from jax import lax
from jax.experimental import pallas as pl
from jax.experimental.pallas import tpu as pltpu
from jax.sharding import PartitionSpec as P

GRID = 64
CHEB = 6
CELLS = GRID * GRID * GRID
PLANES = GRID // 2
DEVICES = 128
MESH_IDS = pl.DeviceIdType.MESH
KINETIC_SCALE = 0.125
SHIFT_VALUE = 0.25
VMEM_LIMIT = 56 * 1024 * 1024
BF16 = jnp.bfloat16
F32 = jnp.float32


def kinetic_taps():
    radius = 14
    values = np.zeros(2 * radius + 1)
    factor = float(math.factorial(radius)) ** 2
    for offset in range(1, radius + 1):
        weight = (
            2.0
            * (-1.0) ** (offset + 1)
            * factor
            / (
                offset
                * offset
                * float(math.factorial(radius - offset))
                * float(math.factorial(radius + offset))
            )
        )
        values[radius + offset] = weight
        values[radius - offset] = weight
    values[radius] = -2.0 * sum((1.0 / float(offset * offset) for offset in range(1, radius + 1)))
    return values


def magic_taps():
    shifted = np.arange(-7, 9) - 0.25
    sinc_values = np.sin(np.pi * shifted) / (np.pi * shifted)
    values = sinc_values * (0.5 + 0.5 * np.cos(np.pi * shifted / 8.5))
    return values / values.sum()


def circulant(values, first, length):
    matrix = np.zeros((length, length))
    for target in range(length):
        for position in range(values.shape[0]):
            matrix[target, (target + first + position) % length] += values[position]
    return matrix


def kinetic_spectrum():
    taps = -KINETIC_SCALE * kinetic_taps()
    offsets = np.arange(-14, 15)
    modes = np.arange(GRID).reshape(GRID, 1)
    return np.cos(2.0 * np.pi * modes * offsets.reshape(1, -1) / GRID) @ taps


def hartley():
    angle = 2.0 * np.pi * np.outer(np.arange(GRID), np.arange(GRID)) / GRID
    return (np.cos(angle) + np.sin(angle)) / np.sqrt(GRID)


def chebyshev_symbol():
    line = kinetic_spectrum()
    low_end = SHIFT_VALUE
    high_end = SHIFT_VALUE + 3.0 * float(line.max())
    centre_value = 0.5 * (high_end + low_end)
    half_width = 0.5 * (high_end - low_end)
    ratio_base = centre_value / half_width
    rho_value = 1.0 / ratio_base
    operator = line[:, None, None] + line[None, :, None] + line[None, None, :] + SHIFT_VALUE
    solution_value = np.zeros_like(operator)
    residual = np.ones_like(operator)
    direction = residual / centre_value
    for counter in range(CHEB):
        solution_value = solution_value + direction
        if counter + 1 < CHEB:
            residual = residual - operator * direction
            rho_next = 1.0 / (2.0 * ratio_base - rho_value)
            direction = rho_next * rho_value * direction + 2.0 * rho_next / half_width * residual
            rho_value = rho_next
    return solution_value.reshape(GRID * PLANES, 128).astype(np.float32)


def split_table(matrix):
    high = np.asarray(matrix, np.float32).astype(jnp.bfloat16)
    low = (np.asarray(matrix, np.float64) - high.astype(np.float64)).astype(np.float32).astype(jnp.bfloat16)
    return high, low


def rows_table(matrix):
    high, low = split_table(matrix)
    return np.concatenate([high, high, low], axis=1)


def lanes_table(*matrices):
    wide = np.concatenate([np.kron(np.eye(2), matrix.T) for matrix in matrices], axis=1)
    high, low = split_table(wide)
    return np.concatenate([high, high, low], axis=0)


def planes_table(matrix):
    even = np.concatenate([matrix[0::2, 0::2], matrix[0::2, 1::2]], axis=1)
    odd = np.concatenate([matrix[1::2, 1::2], matrix[1::2, 0::2]], axis=1)
    return rows_table(np.concatenate([even, odd], axis=0))


def split_pair(value):
    high = value.astype(BF16)
    low = (value - high.astype(F32)).astype(BF16)
    return high, low


def dot32(left, right):
    return jnp.dot(left, right, preferred_element_type=F32)


def along_rows(table, value):
    high, low = split_pair(value)
    return dot32(table, jnp.concatenate([high, low, high], axis=0))


def along_lanes(table, value):
    high, low = split_pair(value)
    return dot32(jnp.concatenate([high, low], axis=1), table[:256]) + dot32(high, table[256:])


def lane_index(shape):
    return lax.broadcasted_iota(jnp.int32, shape, 1)


def plane_stack(value):
    swapped = jnp.concatenate(
        [pltpu.roll(value[:, :128], 64, 1), pltpu.roll(value[:, 128:], 64, 1)], axis=1
    )
    high, low = split_pair(jnp.concatenate([value, swapped], axis=0))
    return jnp.concatenate([high, low, high], axis=0)


def plane_pick(product):
    half = lane_index((PLANES, 256)) % 128 < 64
    return jnp.where(half, product[:PLANES], product[PLANES:])


def two_planes(ref, first):
    return jnp.concatenate(
        [ref[pl.ds(first, PLANES, stride=GRID), :], ref[pl.ds(first + 1, PLANES, stride=GRID), :]],
        axis=1,
    )


def put_two_planes(ref, first, value):
    ref[pl.ds(first, PLANES, stride=GRID), :] = value[:, :128]
    ref[pl.ds(first + 1, PLANES, stride=GRID), :] = value[:, 128:]


def block_of(plane):
    return pl.ds(pl.multiple_of(plane * GRID, GRID), GRID)


def run_bounds(runs):
    row = lax.broadcasted_iota(jnp.int32, (GRID, PLANES), 0)
    column = lax.broadcasted_iota(jnp.int32, (GRID, PLANES), 1)
    repeat = (row // 2 == column).astype(F32).astype(BF16)
    own = lax.broadcasted_iota(jnp.int32, (GRID, 128), 0) % 2 == lane_index((GRID, 128)) // 64
    bounds = []
    for bound in range(2):
        lines = runs[bound : bound + 1, :].reshape(PLANES, 128).astype(F32).astype(BF16)
        bounds.append(jnp.where(own, dot32(repeat, lines), 0.0))
    return jnp.concatenate(bounds, axis=0).astype(BF16)


def region_pair(bounds, pair):
    lane = lane_index((128, 256))
    line = lax.broadcasted_iota(jnp.int32, (128, 256), 0) % GRID
    pick = (line == lane // 64 + 4 * pair).astype(F32).astype(BF16)
    spread = dot32(bounds, pick)
    depth = (lane_index((GRID, 256)) % GRID).astype(F32)
    return ((depth >= spread[:GRID]) & (depth < spread[GRID:])).astype(F32)


def fold_pair(value):
    first, second = value[:, :128], value[:, 128:]
    lower = (lane_index((GRID, 128)) // 32) % 2 == 0
    return jnp.where(lower, first + pltpu.roll(first, 96, 1), second + pltpu.roll(second, 32, 1))


def unfold_pair(tile):
    lower = (lane_index((GRID, 128)) // 32) % 2 == 0
    first = jnp.where(lower, tile, pltpu.roll(tile, 32, 1))
    second = jnp.where(lower, pltpu.roll(tile, 96, 1), tile)
    return jnp.concatenate([first, second], axis=1)


def load_planes(hbm, vmem, sem):
    for plane in range(PLANES):
        pltpu.make_async_copy(
            hbm.at[:, pl.ds(plane * 128, 128)], vmem.at[pl.ds(plane * GRID, GRID), :], sem
        ).start()


def wait_planes(vmem, sem):
    pltpu.make_async_copy(vmem, vmem, sem).wait()


def both_planes(ref, pair):
    return jnp.concatenate([ref[block_of(2 * pair), :], ref[block_of(2 * pair + 1), :]], axis=1)


def put_both_planes(ref, pair, value):
    ref[block_of(2 * pair), :] = value[:, :128]
    ref[block_of(2 * pair + 1), :] = value[:, 128:]


def lanes_pair(table, value):
    stacked = along_lanes(table, jnp.concatenate([value[:, :128], value[:, 128:]], axis=0))
    return stacked[:GRID], stacked[GRID:]


HALF_LOOP = 16


def hamiltonian_head(masked, kinetic, forward, tables, pair, value):
    lanes_kf, rows_k, rows_f = tables
    first, second = lanes_pair(lanes_kf[...], value)
    put_both_planes(masked, pair, value)
    along = jnp.concatenate([first[:, :128], second[:, :128]], axis=1) + along_rows(rows_k[...], value)
    put_both_planes(kinetic, pair, along)
    magic = jnp.concatenate([first[:, 128:], second[:, 128:]], axis=1)
    put_both_planes(forward, pair, along_rows(rows_f[...], magic))


def hamiltonian_middle(masked, kinetic, forward, potential, tables, step):
    planes_k, planes_f, planes_b = tables
    first = 2 * step
    real = plane_pick(dot32(planes_f[...], plane_stack(two_planes(forward, first))))
    weighted = real * two_planes(potential, first)
    put_two_planes(forward, first, plane_pick(dot32(planes_b[...], plane_stack(weighted))))
    along = plane_pick(dot32(planes_k[...], plane_stack(two_planes(masked, first))))
    put_two_planes(kinetic, first, two_planes(kinetic, first) + along)


def hamiltonian_tail(kinetic, forward, tables, pair):
    rows_b, lanes_b = tables
    first, second = lanes_pair(lanes_b[...], along_rows(rows_b[...], both_planes(forward, pair)))
    return both_planes(kinetic, pair) + jnp.concatenate([first, second], axis=1)


def loop(count, body, unroll=1):
    def step(index, carry):
        body(index)
        return carry

    lax.fori_loop(0, count, step, 0, unroll=unroll)


def precondition_kernel(
    tiles, runs, lanes_q, rows_q, planes_q, symbol_hbm, gradient_out, preconditioned_out,
    region, gradient, work, symbol, sems,
):
    fetch = pltpu.make_async_copy(symbol_hbm, symbol, sems.at[0])
    fetch.start()
    bounds = run_bounds(runs[...])

    def put(buffer, target, plane, sem):
        return pltpu.make_async_copy(
            buffer.at[block_of(plane), :],
            target.at[0, :, pl.ds(pl.multiple_of(plane * 128, 128), 128)],
            sem,
        )

    def head(pair):
        mask = region_pair(bounds, pair)
        put_both_planes(region, pair, mask)
        value = unfold_pair(tiles[block_of(pair), :]) * mask
        put_both_planes(gradient, pair, value)
        put(gradient, gradient_out, 2 * pair, sems.at[1]).start()
        put(gradient, gradient_out, 2 * pair + 1, sems.at[1]).start()
        first, second = lanes_pair(lanes_q[...], value)
        put_both_planes(work, pair, along_rows(rows_q[...], jnp.concatenate([first, second], axis=1)))

    loop(PLANES // 2, head, HEAD_UNROLL)
    fetch.wait()

    def middle(step):
        first = 2 * step
        modes = plane_pick(dot32(planes_q[...], plane_stack(two_planes(work, first))))
        factor = jnp.concatenate([symbol[pl.ds(pl.multiple_of(first * PLANES, 64), PLANES), :],
                                  symbol[pl.ds(pl.multiple_of(first * PLANES, 64) + PLANES, PLANES), :]], axis=1)
        put_two_planes(work, first, plane_pick(dot32(planes_q[...], plane_stack(modes * factor))))

    loop(GRID // 2, middle, MIDDLE_UNROLL)
    wait_planes(gradient, sems.at[1])

    def tail(pair):
        first, second = lanes_pair(lanes_q[...], along_rows(rows_q[...], both_planes(work, pair)))
        value = jnp.concatenate([first, second], axis=1) * both_planes(region, pair)
        put_both_planes(work, pair, value)
        put(work, preconditioned_out, 2 * pair, sems.at[2]).start()
        put(work, preconditioned_out, 2 * pair + 1, sems.at[2]).start()

    loop(PLANES // 2, tail, HEAD_UNROLL)
    wait_planes(work, sems.at[2])


HEAD_UNROLL = 4
MIDDLE_UNROLL = 4


def in_vmem(count):
    return [pl.BlockSpec(memory_space=pltpu.VMEM)] * count


def precondition(tiles, line_runs):
    modes = hartley()
    field = pltpu.VMEM((GRID * PLANES, 128), F32)
    shape = jax.ShapeDtypeStruct((1, GRID, GRID * GRID), F32)
    return pl.pallas_call(
        precondition_kernel,
        out_shape=(shape, shape),
        in_specs=in_vmem(5) + [pl.BlockSpec(memory_space=pl.ANY)],
        out_specs=[pl.BlockSpec(memory_space=pl.ANY)] * 2,
        scratch_shapes=[field, field, field, field, pltpu.SemaphoreType.DMA((3,))],
        compiler_params=pltpu.CompilerParams(vmem_limit_bytes=VMEM_LIMIT),
        name="precondition",
    )(
        tiles,
        line_runs,
        jnp.asarray(lanes_table(modes)),
        jnp.asarray(rows_table(modes)),
        jnp.asarray(planes_table(modes)),
        jnp.asarray(chebyshev_symbol()),
    )


def hamiltonian_tables():
    kinetic = -KINETIC_SCALE * circulant(kinetic_taps(), -14, GRID)
    magic = circulant(magic_taps(), -7, GRID)
    tables = (
        lanes_table(kinetic, magic),
        rows_table(kinetic),
        rows_table(magic),
        planes_table(kinetic),
        planes_table(magic),
        planes_table(magic.T),
        rows_table(magic.T),
        lanes_table(magic.T),
    )
    return [jnp.asarray(table) for table in tables]


def tile_of(index):
    return pl.ds(pl.multiple_of(index * 8, 8), 8)


def row_of(index):
    return pl.ds(index, 1)


def peer_id(index):
    return (index // 2, lax.rem(index, 2))


def gradient_kernel(
    wave, potential_hbm, runs, lanes_kf, rows_k, rows_f, planes_k, planes_f, planes_b, rows_b, lanes_b,
    gradient_tiles,
    region, masked, kinetic, forward, potential,
    masked_send, masked_recv, applied_send, applied_recv, back_send,
    partial, gathered, row, matrix,
    load_sems, send_sems, recv_sems,
):
    me = lax.axis_index("orb") * 2 + lax.axis_index("pair")
    barrier = pltpu.get_barrier_semaphore()

    def peer_at(step):
        return lax.rem(me + step, DEVICES)

    def greet(step):
        pl.semaphore_signal(
            barrier, inc=1, device_id=peer_id(peer_at(step + 1)), device_id_type=MESH_IDS
        )

    load_planes(wave.at[0], masked, load_sems.at[0])
    load_planes(potential_hbm, potential, load_sems.at[1])
    loop(DEVICES - 1, greet)
    bounds = run_bounds(runs[...])
    wait_planes(masked, load_sems.at[0])

    def send(source, target, phase, peer, source_at, target_at):
        pltpu.make_async_remote_copy(
            src_ref=source.at[source_at(peer)],
            dst_ref=target.at[target_at(me)],
            send_sem=send_sems.at[phase],
            recv_sem=recv_sems.at[phase],
            device_id=peer_id(peer),
            device_id_type=MESH_IDS,
        ).start()

    def scatter(source, target, phase, source_at, target_at):
        loop(
            DEVICES - 1,
            lambda step: send(source, target, phase, peer_at(step + 1), source_at, target_at),
        )

    def send_tile(source, target, phase, tile):
        @pl.when(tile != me)
        def _():
            send(source, target, phase, tile, tile_of, tile_of)

    def drain(buffer, sem):
        whole = buffer.at[pl.ds(0, buffer.shape[0] * (DEVICES - 1) // DEVICES)]
        pltpu.make_async_copy(whole, whole, sem).wait()

    def head(pair):
        mask = region_pair(bounds, pair)
        put_both_planes(region, pair, mask)
        value = both_planes(masked, pair) * mask
        masked_send[block_of(pair), :] = fold_pair(value)
        hamiltonian_head(masked, kinetic, forward, (lanes_kf, rows_k, rows_f), pair, value)

    loop(PLANES // 2, head, HEAD_UNROLL)
    wait_planes(potential, load_sems.at[1])
    pl.semaphore_wait(barrier, DEVICES - 1)

    def middle(step):
        for sub in range(4):
            send_tile(masked_send, masked_recv, 0, peer_at(4 * step + sub))
        hamiltonian_middle(
            masked, kinetic, forward, potential, (planes_k, planes_f, planes_b), step
        )

    loop(GRID // 2, middle, MIDDLE_UNROLL)
    masked_recv[tile_of(me), :] = masked_send[tile_of(me), :]

    def tail(step):
        pair = lax.rem(step + me // 8, PLANES // 2)
        value = hamiltonian_tail(kinetic, forward, (rows_b, lanes_b), pair) * both_planes(region, pair)
        applied_send[block_of(pair), :] = fold_pair(value)
        for sub in range(8):
            send_tile(applied_send, applied_recv, 1, 8 * pair + lax.rem(me + sub, 8))

    loop(PLANES // 2, tail, TAIL_UNROLL)
    applied_recv[tile_of(me), :] = applied_send[tile_of(me), :]
    drain(masked_recv, recv_sems.at[0])
    drain(applied_recv, recv_sems.at[1])

    total = jnp.zeros((DEVICES, DEVICES), F32)
    for sub in range(8):
        rows = pl.ds(sub, DEVICES, stride=8)
        masked_high, masked_low = split_pair(masked_recv[rows, :])
        applied_high, applied_low = split_pair(applied_recv[rows, :])
        total = total + lax.dot_general(
            jnp.concatenate([applied_high, applied_low], axis=1),
            jnp.concatenate([masked_high, masked_high], axis=1),
            (((1,), (1,)), ((), ())),
            preferred_element_type=F32,
        )
        total = total + lax.dot_general(
            applied_high, masked_low, (((1,), (1,)), ((), ())), preferred_element_type=F32
        )
    partial[:, 0, :] = total
    scatter(partial, gathered, 2, row_of, row_of)
    gathered[row_of(me)] = partial[row_of(me)]
    drain(gathered, recv_sems.at[2])
    row[...] = jnp.sum(gathered[...], axis=0, keepdims=True) * (1.0 / CELLS)
    scatter(row, matrix, 3, lambda peer: pl.ds(0, 1), row_of)
    matrix[row_of(me)] = row[...]
    drain(matrix, recv_sems.at[3])
    matrix_high, matrix_low = split_pair(matrix[:, 0, :])
    table = jnp.concatenate([matrix_high, matrix_low], axis=1)
    for sub in range(8):
        rows = pl.ds(sub, DEVICES, stride=8)
        masked_high, masked_low = split_pair(masked_recv[rows, :])
        projected = dot32(table, jnp.concatenate([masked_high, masked_high], axis=0))
        projected = projected + dot32(matrix_high, masked_low)
        back_send[rows, :] = applied_recv[rows, :] - projected
    scatter(back_send, gradient_tiles, 4, tile_of, tile_of)
    gradient_tiles[tile_of(me), :] = back_send[tile_of(me), :]
    drain(gradient_tiles, recv_sems.at[4])
    drain(masked_send, send_sems.at[0])
    drain(applied_send, send_sems.at[1])
    drain(partial, send_sems.at[2])
    drain(matrix, send_sems.at[3])
    drain(back_send, send_sems.at[4])


TAIL_UNROLL = 1


def gradient_fields(wavefunctions, potential, line_runs):
    field = pltpu.VMEM((GRID * PLANES, 128), F32)
    tiles = pltpu.VMEM((8 * DEVICES, 128), F32)
    rows = pltpu.VMEM((DEVICES, 1, 128), F32)
    return pl.pallas_call(
        gradient_kernel,
        out_shape=jax.ShapeDtypeStruct((8 * DEVICES, 128), F32),
        in_specs=[pl.BlockSpec(memory_space=pl.ANY)] * 2 + in_vmem(9),
        out_specs=pl.BlockSpec(memory_space=pltpu.VMEM),
        scratch_shapes=[
            field, field, field, field, field,
            tiles, tiles, tiles, tiles, tiles,
            rows, rows, pltpu.VMEM((1, 1, 128), F32), rows,
            pltpu.SemaphoreType.DMA((2,)),
            pltpu.SemaphoreType.DMA((5,)),
            pltpu.SemaphoreType.DMA((5,)),
        ],
        compiler_params=pltpu.CompilerParams(
            collective_id=0, has_side_effects=True, vmem_limit_bytes=VMEM_LIMIT
        ),
        name="gradient",
    )(wavefunctions, potential, line_runs, *hamiltonian_tables())


def on_device(wavefunctions, potential, line_runs):
    tiles = gradient_fields(wavefunctions, potential, line_runs)
    return precondition(tiles, line_runs)


def solution(mesh):
    return jax.shard_map(
        on_device,
        mesh=mesh,
        in_specs=(P(("orb", "pair"), None, None), P(), P()),
        out_specs=(P(("orb", "pair"), None, None), P(("orb", "pair"), None, None)),
        check_vma=False,
    )
```

```python
import math

import jax
import jax.numpy as jnp
import numpy as np
from jax import lax
from jax.experimental import pallas as pl
from jax.experimental.pallas import tpu as pltpu
from jax.sharding import PartitionSpec as P

GRID = 64
CHEB = 6
CELLS = GRID * GRID * GRID
PLANES = GRID // 2
DEVICES = 128
MESH_IDS = pl.DeviceIdType.MESH
KINETIC_SCALE = 0.125
SHIFT_VALUE = 0.25
VMEM_LIMIT = 56 * 1024 * 1024
BF16 = jnp.bfloat16
F32 = jnp.float32


def kinetic_taps():
    radius = 14
    values = np.zeros(2 * radius + 1)
    factor = float(math.factorial(radius)) ** 2
    for offset in range(1, radius + 1):
        weight = (
            2.0
            * (-1.0) ** (offset + 1)
            * factor
            / (
                offset
                * offset
                * float(math.factorial(radius - offset))
                * float(math.factorial(radius + offset))
            )
        )
        values[radius + offset] = weight
        values[radius - offset] = weight
    values[radius] = -2.0 * sum((1.0 / float(offset * offset) for offset in range(1, radius + 1)))
    return values


def magic_taps():
    shifted = np.arange(-7, 9) - 0.25
    sinc_values = np.sin(np.pi * shifted) / (np.pi * shifted)
    values = sinc_values * (0.5 + 0.5 * np.cos(np.pi * shifted / 8.5))
    return values / values.sum()


def circulant(values, first, length):
    matrix = np.zeros((length, length))
    for target in range(length):
        for position in range(values.shape[0]):
            matrix[target, (target + first + position) % length] += values[position]
    return matrix


def kinetic_spectrum():
    taps = -KINETIC_SCALE * kinetic_taps()
    offsets = np.arange(-14, 15)
    modes = np.arange(GRID).reshape(GRID, 1)
    return np.cos(2.0 * np.pi * modes * offsets.reshape(1, -1) / GRID) @ taps


def hartley():
    angle = 2.0 * np.pi * np.outer(np.arange(GRID), np.arange(GRID)) / GRID
    return (np.cos(angle) + np.sin(angle)) / np.sqrt(GRID)


def chebyshev_symbol():
    line = kinetic_spectrum()
    low_end = SHIFT_VALUE
    high_end = SHIFT_VALUE + 3.0 * float(line.max())
    centre_value = 0.5 * (high_end + low_end)
    half_width = 0.5 * (high_end - low_end)
    ratio_base = centre_value / half_width
    rho_value = 1.0 / ratio_base
    operator = line[:, None, None] + line[None, :, None] + line[None, None, :] + SHIFT_VALUE
    solution_value = np.zeros_like(operator)
    residual = np.ones_like(operator)
    direction = residual / centre_value
    for counter in range(CHEB):
        solution_value = solution_value + direction
        if counter + 1 < CHEB:
            residual = residual - operator * direction
            rho_next = 1.0 / (2.0 * ratio_base - rho_value)
            direction = rho_next * rho_value * direction + 2.0 * rho_next / half_width * residual
            rho_value = rho_next
    blocks = solution_value.reshape(GRID // 4, 2, 2, PLANES, 2, GRID)
    return blocks.transpose(0, 4, 3, 1, 2, 5).reshape(GRID // 4 * GRID, 256).astype(np.float32)


def split_table(matrix):
    high = np.asarray(matrix, np.float32).astype(jnp.bfloat16)
    low = (np.asarray(matrix, np.float64) - high.astype(np.float64)).astype(np.float32).astype(jnp.bfloat16)
    return high, low


def rows_table(matrix):
    high, low = split_table(matrix)
    return np.concatenate([high, high, low], axis=1)


def columns_table(matrix):
    order = np.concatenate([np.arange(0, GRID, 2), np.arange(1, GRID, 2)])
    return rows_table(matrix[order][:, order])


def lanes_table(matrix):
    high, low = split_table(np.kron(np.eye(2), matrix.T))
    both = np.concatenate([high, low], axis=1)
    return np.concatenate([both, both], axis=0)


def lanes_table_of_two(first, second):
    parts = [split_table(np.kron(np.eye(2), matrix.T)) for matrix in (first, second)]
    high = np.concatenate([part[0] for part in parts], axis=1)
    low = np.concatenate([part[1] for part in parts], axis=1)
    return np.concatenate([high, high, low], axis=0)


def split_pair(value):
    high = value.astype(BF16)
    low = (value - high.astype(F32)).astype(BF16)
    return high, low


def dot32(left, right):
    return jnp.dot(left, right, preferred_element_type=F32)


def along_rows(table, value):
    high, low = split_pair(value)
    return dot32(table, jnp.concatenate([high, low, high], axis=0))


def along_lanes(table, value):
    high, low = split_pair(value)
    product = dot32(jnp.concatenate([high, low], axis=1), table)
    return product[:, :128] + product[:, 128:]


def along_lanes_of_two(table, value):
    high, low = split_pair(value)
    product = dot32(jnp.concatenate([high, low, high], axis=1), table)
    return product[:, :128], product[:, 128:]


def lane_index(shape):
    return lax.broadcasted_iota(jnp.int32, shape, 1)


PITCH = GRID + 1
PITCHED = (PITCH * PLANES, 128)


def x_rows(first):
    return pl.ds(first, PLANES, stride=PITCH)


def turn(first, second):
    half = lane_index((PLANES, 128)) < 64
    return (
        jnp.where(half, first, pltpu.roll(second, 64, 1)),
        jnp.where(half, pltpu.roll(first, 64, 1), second),
    )


def columns_of(ref, first):
    pairs = [
        jnp.concatenate(turn(ref[x_rows(first + shift), :], ref[x_rows(first + shift + 1), :]), axis=0)
        for shift in (0, 2)
    ]
    return jnp.concatenate(pairs, axis=1)


def x_planes(value):
    return (
        *turn(value[:PLANES, :128], value[PLANES:, :128]),
        *turn(value[:PLANES, 128:], value[PLANES:, 128:]),
    )


def put_columns(ref, first, value):
    for shift, plane in enumerate(x_planes(value)):
        ref[x_rows(first + shift), :] = plane


def add_columns(ref, first, value):
    for shift, plane in enumerate(x_planes(value)):
        ref[x_rows(first + shift), :] = ref[x_rows(first + shift), :] + plane


def block_of(plane):
    return pl.ds(pl.multiple_of(plane * GRID, GRID), GRID)


def run_bounds(runs):
    row = lax.broadcasted_iota(jnp.int32, (GRID, PLANES), 0)
    column = lax.broadcasted_iota(jnp.int32, (GRID, PLANES), 1)
    repeat = (row // 2 == column).astype(F32).astype(BF16)
    own = lax.broadcasted_iota(jnp.int32, (GRID, 128), 0) % 2 == lane_index((GRID, 128)) // 64
    bounds = []
    for bound in range(2):
        lines = runs[bound : bound + 1, :].reshape(PLANES, 128).astype(F32).astype(BF16)
        bounds.append(jnp.where(own, dot32(repeat, lines), 0.0))
    return jnp.concatenate(bounds, axis=0).astype(BF16)


def region_pair(bounds, pair):
    lane = lane_index((128, 256))
    line = lax.broadcasted_iota(jnp.int32, (128, 256), 0) % GRID
    pick = (line == lane // 64 + 4 * pair).astype(F32).astype(BF16)
    spread = dot32(bounds, pick)
    depth = (lane_index((GRID, 256)) % GRID).astype(F32)
    return ((depth >= spread[:GRID]) & (depth < spread[GRID:])).astype(F32)


def fold_pair(value):
    first, second = value[:, :128], value[:, 128:]
    lower = (lane_index((GRID, 128)) // 32) % 2 == 0
    return jnp.where(lower, first + pltpu.roll(first, 96, 1), second + pltpu.roll(second, 32, 1))


def unfold_pair(tile):
    lower = (lane_index((GRID, 128)) // 32) % 2 == 0
    first = jnp.where(lower, tile, pltpu.roll(tile, 32, 1))
    second = jnp.where(lower, pltpu.roll(tile, 96, 1), tile)
    return jnp.concatenate([first, second], axis=1)


def load_planes(hbm, vmem, sem):
    for plane in range(PLANES):
        pltpu.make_async_copy(
            hbm.at[:, pl.ds(plane * 128, 128)], vmem.at[pl.ds(plane * GRID, GRID), :], sem
        ).start()


def wait_planes(vmem, sem):
    pltpu.make_async_copy(vmem, vmem, sem).wait()


def pitched_block(plane):
    return pl.ds(plane * PITCH, GRID)


def both_planes(ref, pair, at=pitched_block):
    return jnp.concatenate([ref[at(2 * pair), :], ref[at(2 * pair + 1), :]], axis=1)


def put_both_planes(ref, pair, value, at=pitched_block):
    ref[at(2 * pair), :] = value[:, :128]
    ref[at(2 * pair + 1), :] = value[:, 128:]


def stacked(values):
    return jnp.concatenate([half for value in values for half in (value[:, :128], value[:, 128:])], axis=0)


def unstacked(value):
    return [
        jnp.concatenate([value[row : row + GRID], value[row + GRID : row + 2 * GRID]], axis=1)
        for row in range(0, value.shape[0], 2 * GRID)
    ]


GROUP = 4
GROUPS = PLANES // 2 // GROUP


def pairs_of(group):
    return [group * GROUP + member for member in range(GROUP)]


def hamiltonian_head(kinetic, forward, tables, group, values):
    lanes_kf, rows_k, rows_f = tables
    along, magic = along_lanes_of_two(lanes_kf[...], stacked(values))
    for pair, value, first, second in zip(pairs_of(group), values, unstacked(along), unstacked(magic)):
        put_both_planes(kinetic, pair, first + along_rows(rows_k[...], value))
        put_both_planes(forward, pair, along_rows(rows_f[...], second))


def hamiltonian_middle(masked, kinetic, forward, potential, tables, step):
    columns_k, columns_f, columns_b = tables
    first = 4 * step
    real = along_rows(columns_f[...], columns_of(forward, first))
    weighted = real * columns_of(potential, first)
    put_columns(forward, first, along_rows(columns_b[...], weighted))
    add_columns(kinetic, first, along_rows(columns_k[...], columns_of(masked, first)))


def hamiltonian_tail(kinetic, forward, tables, group):
    rows_b, lanes_b = tables
    values = [along_rows(rows_b[...], both_planes(forward, pair)) for pair in pairs_of(group)]
    returned = unstacked(along_lanes(lanes_b[...], stacked(values)))
    return [both_planes(kinetic, pair) + value for pair, value in zip(pairs_of(group), returned)]


def loop(count, body, unroll=1):
    def step(index, carry):
        body(index)
        return carry

    lax.fori_loop(0, count, step, 0, unroll=unroll)


def precondition_kernel(
    tiles_hbm, region_hbm, lanes_q, rows_q, columns_q, symbol_hbm, gradient_out, preconditioned_out,
    tiles, region, gradient, work, symbol, load_sems, sems,
):
    def fetch(group):
        rows = pl.ds(group * GROUP * GRID, GROUP * GRID)
        planes = pl.ds(group * GROUP * 2 * GRID, GROUP * 2 * GRID)
        return (
            pltpu.make_async_copy(tiles_hbm.at[rows], tiles.at[rows], load_sems.at[0, group]),
            pltpu.make_async_copy(region_hbm.at[planes], region.at[planes], load_sems.at[1, group]),
        )

    for group in range(GROUPS):
        for copy in fetch(group):
            copy.start()
    symbol_copy = pltpu.make_async_copy(symbol_hbm, symbol, sems.at[0])
    symbol_copy.start()

    def put(buffer, target, pair, sem):
        for plane in (2 * pair, 2 * pair + 1):
            pltpu.make_async_copy(
                buffer.at[block_of(plane), :],
                target.at[0, :, pl.ds(pl.multiple_of(plane * 128, 128), 128)],
                sem,
            ).start()

    def head(group):
        for copy in fetch(group):
            copy.wait()
        values = []
        for pair in pairs_of(group):
            value = unfold_pair(tiles[block_of(pair), :]) * both_planes(region, pair, block_of)
            put_both_planes(gradient, pair, value, block_of)
            put(gradient, gradient_out, pair, sems.at[1])
            values.append(value)
        turned = unstacked(along_lanes(lanes_q[...], stacked(values)))
        for pair, value in zip(pairs_of(group), turned):
            put_both_planes(work, pair, along_rows(rows_q[...], value))

    loop(GROUPS, head)
    symbol_copy.wait()

    def middle(step):
        first = 4 * step
        modes = along_rows(columns_q[...], columns_of(work, first)) * symbol[block_of(step), :]
        put_columns(work, first, along_rows(columns_q[...], modes))

    loop(GRID // 4, middle, MIDDLE_UNROLL)
    wait_planes(gradient, sems.at[1])

    def tail(group):
        values = [along_rows(rows_q[...], both_planes(work, pair)) for pair in pairs_of(group)]
        turned = unstacked(along_lanes(lanes_q[...], stacked(values)))
        for pair, value in zip(pairs_of(group), turned):
            put_both_planes(gradient, pair, value * both_planes(region, pair, block_of), block_of)
            put(gradient, preconditioned_out, pair, sems.at[2])

    loop(GROUPS, tail)
    wait_planes(gradient, sems.at[2])


MIDDLE_UNROLL = 2


def in_vmem(count):
    return [pl.BlockSpec(memory_space=pltpu.VMEM)] * count


def anywhere(count):
    return [pl.BlockSpec(memory_space=pl.ANY)] * count


FIELD = (GRID * PLANES, 128)
TILES = (8 * DEVICES, 128)


def precondition(tiles, region):
    modes = hartley()
    field = pltpu.VMEM(FIELD, F32)
    pitched = pltpu.VMEM(PITCHED, F32)
    shape = jax.ShapeDtypeStruct((1, GRID, GRID * GRID), F32)
    return pl.pallas_call(
        precondition_kernel,
        out_shape=(shape, shape),
        in_specs=anywhere(2) + in_vmem(3) + anywhere(1),
        out_specs=anywhere(2),
        scratch_shapes=[
            pltpu.VMEM(TILES, F32), field, field, pitched, pltpu.VMEM((GRID // 4 * GRID, 256), F32),
            pltpu.SemaphoreType.DMA((2, GROUPS)),
            pltpu.SemaphoreType.DMA((3,)),
        ],
        compiler_params=pltpu.CompilerParams(vmem_limit_bytes=VMEM_LIMIT),
        name="precondition",
    )(
        tiles,
        region,
        jnp.asarray(lanes_table(modes)),
        jnp.asarray(rows_table(modes)),
        jnp.asarray(columns_table(modes)),
        jnp.asarray(chebyshev_symbol()),
    )


def hamiltonian_tables():
    kinetic = -KINETIC_SCALE * circulant(kinetic_taps(), -14, GRID)
    magic = circulant(magic_taps(), -7, GRID)
    tables = (
        lanes_table_of_two(kinetic, magic),
        rows_table(kinetic),
        rows_table(magic),
        columns_table(kinetic),
        columns_table(magic),
        columns_table(magic.T),
        rows_table(magic.T),
        lanes_table(magic.T),
    )
    return [jnp.asarray(table) for table in tables]


def tile_of(index):
    return pl.ds(pl.multiple_of(index * 8, 8), 8)


def row_of(index):
    return pl.ds(index, 1)


def gradient_kernel(
    wave, potential_hbm, runs, lanes_kf, rows_k, rows_f, columns_k, columns_f, columns_b, rows_b, lanes_b,
    gradient_tiles, region_out,
    waves, staged, region, masked, kinetic, forward, potential,
    masked_send, masked_recv, applied_send, applied_recv, back_send,
    partial, gathered, row, matrix,
    load_sems, send_sems, recv_sems,
):
    me = lax.axis_index("orb") * 2 + lax.axis_index("pair")
    barrier = pltpu.get_barrier_semaphore()

    def peer_at(step):
        return jnp.bitwise_and(me + step, DEVICES - 1)

    def greet(step):
        pl.semaphore_signal(barrier, inc=1, device_id=peer_at(step + 1), device_id_type=LOGICAL)

    load_planes(wave.at[0], waves, load_sems.at[0])
    loop(DEVICES - 1, greet, SEND_UNROLL)
    load_planes(potential_hbm, staged, load_sems.at[1])
    bounds = run_bounds(runs[...])
    wait_planes(waves, load_sems.at[0])

    def send(source, target, phase, peer, source_at, target_at):
        pltpu.make_async_remote_copy(
            src_ref=source.at[source_at(peer)],
            dst_ref=target.at[target_at(me)],
            send_sem=send_sems.at[phase],
            recv_sem=recv_sems.at[phase],
            device_id=peer,
            device_id_type=LOGICAL,
        ).start()

    def scatter(source, target, phase, source_at, target_at):
        loop(
            DEVICES - 1,
            lambda step: send(source, target, phase, peer_at(step + 1), source_at, target_at),
            SEND_UNROLL,
        )

    def drain(buffer, sem):
        whole = buffer.at[pl.ds(0, buffer.shape[0] * (DEVICES - 1) // DEVICES)]
        pltpu.make_async_copy(whole, whole, sem).wait()

    def head(group):
        values = []
        for pair in pairs_of(group):
            mask = region_pair(bounds, pair)
            put_both_planes(region, pair, mask, block_of)
            value = both_planes(waves, pair, block_of) * mask
            put_both_planes(masked, pair, value)
            masked_send[block_of(pair), :] = fold_pair(value)
            values.append(value)
        hamiltonian_head(kinetic, forward, (lanes_kf, rows_k, rows_f), group, values)

    loop(GROUPS, head)
    region_copy = pltpu.make_async_copy(region, region_out, load_sems.at[2])
    region_copy.start()
    wait_planes(staged, load_sems.at[1])

    def pitch(pair):
        put_both_planes(potential, pair, both_planes(staged, pair, block_of))

    loop(PLANES // 2, pitch, 4)
    pl.semaphore_wait(barrier, DEVICES - 1)

    def middle(step):
        hamiltonian_middle(
            masked, kinetic, forward, potential, (columns_k, columns_f, columns_b), step
        )

    def middle_sending(step):
        for sub in range(9):
            send(masked_send, masked_recv, 0, peer_at(9 * step + sub + 1), tile_of, tile_of)
        middle(step)

    loop(14, middle_sending, MIDDLE_UNROLL)
    send(masked_send, masked_recv, 0, peer_at(127), tile_of, tile_of)
    middle(14)
    middle(15)
    masked_recv[tile_of(me), :] = masked_send[tile_of(me), :]

    def tail(step, sends):
        group = jnp.bitwise_and(lax.shift_right_logical(me, GROUP_SHIFT) + (step + 1), GROUPS - 1)
        values = hamiltonian_tail(kinetic, forward, (rows_b, lanes_b), group)
        for pair, value in zip(pairs_of(group), values):
            applied_send[block_of(pair), :] = fold_pair(value * both_planes(region, pair, block_of))
        for sub in range(sends):
            peer = 8 * GROUP * group + jnp.bitwise_and(me + (sub + 1), 8 * GROUP - 1)
            send(applied_send, applied_recv, 1, peer, tile_of, tile_of)

    loop(GROUPS - 1, lambda step: tail(step, 8 * GROUP))
    tail(GROUPS - 1, 8 * GROUP - 1)
    applied_recv[tile_of(me), :] = applied_send[tile_of(me), :]
    drain(masked_recv, recv_sems.at[0])
    drain(applied_recv, recv_sems.at[1])

    total = jnp.zeros((2 * DEVICES, 2 * DEVICES), F32)
    for sub in range(0, 8, 2):
        left = []
        right = []
        for one in (sub, sub + 1):
            rows = pl.ds(one, DEVICES, stride=8)
            left.append(jnp.concatenate(split_pair(applied_recv[rows, :]), axis=0))
            right.append(jnp.concatenate(split_pair(masked_recv[rows, :]), axis=0))
        total = total + lax.dot_general(
            jnp.concatenate(left, axis=1),
            jnp.concatenate(right, axis=1),
            (((1,), (1,)), ((), ())),
            preferred_element_type=F32,
        )
    partial[:, 0, :] = (
        total[:DEVICES, :DEVICES] + (total[:DEVICES, DEVICES:] + total[DEVICES:, :DEVICES])
    )
    scatter(partial, gathered, 2, row_of, row_of)
    gathered[row_of(me)] = partial[row_of(me)]
    drain(gathered, recv_sems.at[2])
    row[...] = jnp.sum(gathered[...], axis=0, keepdims=True) * (1.0 / CELLS)
    scatter(row, matrix, 3, lambda peer: pl.ds(0, 1), row_of)
    matrix[row_of(me)] = row[...]
    drain(matrix, recv_sems.at[3])
    matrix_high, matrix_low = split_pair(matrix[:, 0, :])
    table = jnp.concatenate([matrix_high, matrix_high, matrix_low], axis=1)
    for sub in range(0, 8, 2):
        here = pl.ds(sub, DEVICES, stride=8)
        there = pl.ds(sub + 1, DEVICES, stride=8)
        projected = along_rows(
            table, jnp.concatenate([masked_recv[here, :], masked_recv[there, :]], axis=1)
        )
        back_send[here, :] = applied_recv[here, :] - projected[:, :128]
        back_send[there, :] = applied_recv[there, :] - projected[:, 128:]
    scatter(back_send, gradient_tiles, 4, tile_of, tile_of)
    gradient_tiles[tile_of(me), :] = back_send[tile_of(me), :]
    region_copy.wait()
    drain(masked_send, send_sems.at[0])
    drain(applied_send, send_sems.at[1])
    drain(partial, send_sems.at[2])
    drain(matrix, send_sems.at[3])
    drain(gradient_tiles, recv_sems.at[4])
    drain(back_send, send_sems.at[4])


SEND_UNROLL = 8
GROUP_SHIFT = 5
LOGICAL = pl.DeviceIdType.LOGICAL


def gradient_fields(wavefunctions, potential, line_runs):
    field = pltpu.VMEM(FIELD, F32)
    pitched = pltpu.VMEM(PITCHED, F32)
    tiles = pltpu.VMEM(TILES, F32)
    rows = pltpu.VMEM((DEVICES, 1, 128), F32)
    return pl.pallas_call(
        gradient_kernel,
        out_shape=(jax.ShapeDtypeStruct(TILES, F32), jax.ShapeDtypeStruct(FIELD, F32)),
        in_specs=anywhere(2) + in_vmem(9),
        out_specs=in_vmem(1) + anywhere(1),
        scratch_shapes=[
            field, field, field, pitched, pitched, pitched, pitched,
            tiles, tiles, tiles, tiles, tiles,
            rows, rows, pltpu.VMEM((1, 1, 128), F32), rows,
            pltpu.SemaphoreType.DMA((3,)),
            pltpu.SemaphoreType.DMA((5,)),
            pltpu.SemaphoreType.DMA((5,)),
        ],
        compiler_params=pltpu.CompilerParams(
            collective_id=0, has_side_effects=True, vmem_limit_bytes=VMEM_LIMIT
        ),
        name="gradient",
    )(wavefunctions, potential, line_runs, *hamiltonian_tables())


def on_device(wavefunctions, potential, line_runs):
    tiles, region = gradient_fields(wavefunctions, potential, line_runs)
    return precondition(tiles, region)


def solution(mesh):
    return jax.shard_map(
        on_device,
        mesh=mesh,
        in_specs=(P(("orb", "pair"), None, None), P(), P()),
        out_specs=(P(("orb", "pair"), None, None), P(("orb", "pair"), None, None)),
        check_vma=False,
    )
```

```python
import math

import jax
import jax.numpy as jnp
import numpy as np
from jax import lax
from jax.experimental import pallas as pl
from jax.experimental.pallas import tpu as pltpu
from jax.sharding import PartitionSpec as P

GRID = 64
CHEB = 6
CELLS = GRID * GRID * GRID
PLANES = GRID // 2
DEVICES = 128
KINETIC_SCALE = 0.125
SHIFT_VALUE = 0.25
VMEM_LIMIT = 56 * 1024 * 1024
BF16 = jnp.bfloat16
F32 = jnp.float32


def kinetic_taps():
    radius = 14
    values = np.zeros(2 * radius + 1)
    factor = float(math.factorial(radius)) ** 2
    for offset in range(1, radius + 1):
        weight = (
            2.0
            * (-1.0) ** (offset + 1)
            * factor
            / (
                offset
                * offset
                * float(math.factorial(radius - offset))
                * float(math.factorial(radius + offset))
            )
        )
        values[radius + offset] = weight
        values[radius - offset] = weight
    values[radius] = -2.0 * sum((1.0 / float(offset * offset) for offset in range(1, radius + 1)))
    return values


def magic_taps():
    shifted = np.arange(-7, 9) - 0.25
    sinc_values = np.sin(np.pi * shifted) / (np.pi * shifted)
    values = sinc_values * (0.5 + 0.5 * np.cos(np.pi * shifted / 8.5))
    return values / values.sum()


def circulant(values, first, length):
    matrix = np.zeros((length, length))
    for target in range(length):
        for position in range(values.shape[0]):
            matrix[target, (target + first + position) % length] += values[position]
    return matrix


def kinetic_spectrum():
    taps = -KINETIC_SCALE * kinetic_taps()
    offsets = np.arange(-14, 15)
    modes = np.arange(GRID).reshape(GRID, 1)
    return np.cos(2.0 * np.pi * modes * offsets.reshape(1, -1) / GRID) @ taps


def hartley():
    angle = 2.0 * np.pi * np.outer(np.arange(GRID), np.arange(GRID)) / GRID
    return (np.cos(angle) + np.sin(angle)) / np.sqrt(GRID)


def chebyshev_symbol():
    line = kinetic_spectrum()
    low_end = SHIFT_VALUE
    high_end = SHIFT_VALUE + 3.0 * float(line.max())
    centre_value = 0.5 * (high_end + low_end)
    half_width = 0.5 * (high_end - low_end)
    ratio_base = centre_value / half_width
    rho_value = 1.0 / ratio_base
    operator = line[:, None, None] + line[None, :, None] + line[None, None, :] + SHIFT_VALUE
    solution_value = np.zeros_like(operator)
    residual = np.ones_like(operator)
    direction = residual / centre_value
    for counter in range(CHEB):
        solution_value = solution_value + direction
        if counter + 1 < CHEB:
            residual = residual - operator * direction
            rho_next = 1.0 / (2.0 * ratio_base - rho_value)
            direction = rho_next * rho_value * direction + 2.0 * rho_next / half_width * residual
            rho_value = rho_next
    blocks = solution_value.reshape(GRID // 4, 2, 2, PLANES, 2, GRID)
    return blocks.transpose(0, 4, 3, 1, 2, 5).reshape(GRID // 4 * GRID, 256).astype(np.float32)


def split_table(matrix):
    high = np.asarray(matrix, np.float32).astype(jnp.bfloat16)
    low = (np.asarray(matrix, np.float64) - high.astype(np.float64)).astype(np.float32).astype(jnp.bfloat16)
    return high, low


def rows_table(matrix):
    high, low = split_table(matrix)
    return np.concatenate([high, high, low], axis=1)


def columns_table(matrix):
    order = np.concatenate([np.arange(0, GRID, 2), np.arange(1, GRID, 2)])
    return rows_table(matrix[order][:, order])


def lanes_table(matrix):
    high, low = split_table(np.kron(np.eye(2), matrix.T))
    both = np.concatenate([high, low], axis=1)
    return np.concatenate([both, both], axis=0)


def lanes_table_of_two(first, second):
    parts = [split_table(np.kron(np.eye(2), matrix.T)) for matrix in (first, second)]
    high = np.concatenate([part[0] for part in parts], axis=1)
    low = np.concatenate([part[1] for part in parts], axis=1)
    return np.concatenate([high, high, low], axis=0)


def split_pair(value):
    high = value.astype(BF16)
    low = (value - high.astype(F32)).astype(BF16)
    return high, low


def dot32(left, right):
    return jnp.dot(left, right, preferred_element_type=F32)


def along_rows(table, value):
    high, low = split_pair(value)
    return dot32(table, jnp.concatenate([high, low, high], axis=0))


def along_lanes(table, value):
    high, low = split_pair(value)
    product = dot32(jnp.concatenate([high, low], axis=1), table)
    return product[:, :128] + product[:, 128:]


def along_lanes_of_two(table, value):
    high, low = split_pair(value)
    product = dot32(jnp.concatenate([high, low, high], axis=1), table)
    return product[:, :128], product[:, 128:]


def lane_index(shape):
    return lax.broadcasted_iota(jnp.int32, shape, 1)


PITCH = GRID + 1
PITCHED = (PITCH * PLANES, 128)


def x_rows(first):
    return pl.ds(first, PLANES, stride=PITCH)


def turn(first, second):
    half = lane_index((PLANES, 128)) < 64
    return (
        jnp.where(half, first, pltpu.roll(second, 64, 1)),
        jnp.where(half, pltpu.roll(first, 64, 1), second),
    )


def columns_of(ref, first):
    pairs = [
        jnp.concatenate(turn(ref[x_rows(first + shift), :], ref[x_rows(first + shift + 1), :]), axis=0)
        for shift in (0, 2)
    ]
    return jnp.concatenate(pairs, axis=1)


def x_planes(value):
    return (
        *turn(value[:PLANES, :128], value[PLANES:, :128]),
        *turn(value[:PLANES, 128:], value[PLANES:, 128:]),
    )


def put_columns(ref, first, value):
    for shift, plane in enumerate(x_planes(value)):
        ref[x_rows(first + shift), :] = plane


def add_columns(ref, first, value):
    for shift, plane in enumerate(x_planes(value)):
        ref[x_rows(first + shift), :] = ref[x_rows(first + shift), :] + plane


def block_of(plane):
    return pl.ds(pl.multiple_of(plane * GRID, GRID), GRID)


def run_bounds(runs):
    row = lax.broadcasted_iota(jnp.int32, (GRID, PLANES), 0)
    column = lax.broadcasted_iota(jnp.int32, (GRID, PLANES), 1)
    repeat = (row // 2 == column).astype(F32).astype(BF16)
    own = lax.broadcasted_iota(jnp.int32, (GRID, 128), 0) % 2 == lane_index((GRID, 128)) // 64
    bounds = []
    for bound in range(2):
        lines = runs[bound : bound + 1, :].reshape(PLANES, 128).astype(F32).astype(BF16)
        bounds.append(jnp.where(own, dot32(repeat, lines), 0.0))
    return jnp.concatenate(bounds, axis=0).astype(BF16)


def region_pair(bounds, pair):
    lane = lane_index((128, 256))
    line = lax.broadcasted_iota(jnp.int32, (128, 256), 0) % GRID
    pick = (line == lane // 64 + 4 * pair).astype(F32).astype(BF16)
    spread = dot32(bounds, pick)
    depth = (lane_index((GRID, 256)) % GRID).astype(F32)
    return ((depth >= spread[:GRID]) & (depth < spread[GRID:])).astype(F32)


def fold_pair(value):
    first, second = value[:, :128], value[:, 128:]
    lower = (lane_index((GRID, 128)) // 32) % 2 == 0
    return jnp.where(lower, first + pltpu.roll(first, 96, 1), second + pltpu.roll(second, 32, 1))


def unfold_pair(tile):
    lower = (lane_index((GRID, 128)) // 32) % 2 == 0
    first = jnp.where(lower, tile, pltpu.roll(tile, 32, 1))
    second = jnp.where(lower, pltpu.roll(tile, 96, 1), tile)
    return jnp.concatenate([first, second], axis=1)


def load_planes(hbm, vmem, sem):
    for plane in range(PLANES):
        pltpu.make_async_copy(
            hbm.at[:, pl.ds(plane * 128, 128)], vmem.at[pl.ds(plane * GRID, GRID), :], sem
        ).start()


def wait_planes(vmem, sem):
    pltpu.make_async_copy(vmem, vmem, sem).wait()


def pitched_block(plane):
    return pl.ds(plane * PITCH, GRID)


def both_planes(ref, pair, at=pitched_block):
    return jnp.concatenate([ref[at(2 * pair), :], ref[at(2 * pair + 1), :]], axis=1)


def put_both_planes(ref, pair, value, at=pitched_block):
    ref[at(2 * pair), :] = value[:, :128]
    ref[at(2 * pair + 1), :] = value[:, 128:]


def stacked(values):
    return jnp.concatenate([half for value in values for half in (value[:, :128], value[:, 128:])], axis=0)


def unstacked(value):
    return [
        jnp.concatenate([value[row : row + GRID], value[row + GRID : row + 2 * GRID]], axis=1)
        for row in range(0, value.shape[0], 2 * GRID)
    ]


GROUP = 4
GROUPS = PLANES // 2 // GROUP


def pairs_of(group):
    return [group * GROUP + member for member in range(GROUP)]


def hamiltonian_head(kinetic, forward, tables, group, values):
    lanes_kf, rows_k, rows_f = tables
    along, magic = along_lanes_of_two(lanes_kf[...], stacked(values))
    for pair, value, first, second in zip(pairs_of(group), values, unstacked(along), unstacked(magic)):
        put_both_planes(kinetic, pair, first + along_rows(rows_k[...], value))
        put_both_planes(forward, pair, along_rows(rows_f[...], second))


def hamiltonian_middle(masked, kinetic, forward, potential, tables, step):
    columns_k, columns_f, columns_b = tables
    first = 4 * step
    real = along_rows(columns_f[...], columns_of(forward, first))
    weighted = real * columns_of(potential, first)
    put_columns(forward, first, along_rows(columns_b[...], weighted))
    add_columns(kinetic, first, along_rows(columns_k[...], columns_of(masked, first)))


def hamiltonian_tail(kinetic, forward, tables, group):
    rows_b, lanes_b = tables
    values = [along_rows(rows_b[...], both_planes(forward, pair)) for pair in pairs_of(group)]
    returned = unstacked(along_lanes(lanes_b[...], stacked(values)))
    return [both_planes(kinetic, pair) + value for pair, value in zip(pairs_of(group), returned)]


def loop(count, body, unroll=1):
    def step(index, carry):
        body(index)
        return carry

    lax.fori_loop(0, count, step, 0, unroll=unroll)


def precondition_kernel(
    tiles_hbm, region_hbm, lanes_q, rows_q, columns_q, symbol_hbm, gradient_out, preconditioned_out,
    tiles, region, gradient, work, symbol, load_sems, sems,
):
    def fetch(group):
        rows = pl.ds(group * GROUP * GRID, GROUP * GRID)
        planes = pl.ds(group * GROUP * 2 * GRID, GROUP * 2 * GRID)
        return (
            pltpu.make_async_copy(tiles_hbm.at[rows], tiles.at[rows], load_sems.at[0, group]),
            pltpu.make_async_copy(region_hbm.at[planes], region.at[planes], load_sems.at[1, group]),
        )

    for group in range(GROUPS):
        for copy in fetch(group):
            copy.start()
    symbol_copy = pltpu.make_async_copy(symbol_hbm, symbol, sems.at[0])
    symbol_copy.start()

    def put(buffer, target, pair, sem):
        for plane in (2 * pair, 2 * pair + 1):
            pltpu.make_async_copy(
                buffer.at[block_of(plane), :],
                target.at[0, :, pl.ds(pl.multiple_of(plane * 128, 128), 128)],
                sem,
            ).start()

    def head(group):
        for copy in fetch(group):
            copy.wait()
        values = []
        for pair in pairs_of(group):
            value = unfold_pair(tiles[block_of(pair), :]) * both_planes(region, pair, block_of)
            put_both_planes(gradient, pair, value, block_of)
            put(gradient, gradient_out, pair, sems.at[1])
            values.append(value)
        turned = unstacked(along_lanes(lanes_q[...], stacked(values)))
        for pair, value in zip(pairs_of(group), turned):
            put_both_planes(work, pair, along_rows(rows_q[...], value))

    loop(GROUPS, head)
    symbol_copy.wait()

    def middle(step):
        first = 4 * step
        modes = along_rows(columns_q[...], columns_of(work, first)) * symbol[block_of(step), :]
        put_columns(work, first, along_rows(columns_q[...], modes))

    loop(GRID // 4, middle, MIDDLE_UNROLL)
    wait_planes(gradient, sems.at[1])

    def tail(group):
        values = [along_rows(rows_q[...], both_planes(work, pair)) for pair in pairs_of(group)]
        turned = unstacked(along_lanes(lanes_q[...], stacked(values)))
        for pair, value in zip(pairs_of(group), turned):
            put_both_planes(gradient, pair, value * both_planes(region, pair, block_of), block_of)
            put(gradient, preconditioned_out, pair, sems.at[2])

    loop(GROUPS, tail)
    wait_planes(gradient, sems.at[2])


MIDDLE_UNROLL = 2


def in_vmem(count):
    return [pl.BlockSpec(memory_space=pltpu.VMEM)] * count


def anywhere(count):
    return [pl.BlockSpec(memory_space=pl.ANY)] * count


FIELD = (GRID * PLANES, 128)
TILES = (8 * DEVICES, 128)


def precondition(tiles, region):
    modes = hartley()
    field = pltpu.VMEM(FIELD, F32)
    pitched = pltpu.VMEM(PITCHED, F32)
    shape = jax.ShapeDtypeStruct((1, GRID, GRID * GRID), F32)
    return pl.pallas_call(
        precondition_kernel,
        out_shape=(shape, shape),
        in_specs=anywhere(2) + in_vmem(3) + anywhere(1),
        out_specs=anywhere(2),
        scratch_shapes=[
            pltpu.VMEM(TILES, F32), field, field, pitched, pltpu.VMEM((GRID // 4 * GRID, 256), F32),
            pltpu.SemaphoreType.DMA((2, GROUPS)),
            pltpu.SemaphoreType.DMA((3,)),
        ],
        compiler_params=pltpu.CompilerParams(vmem_limit_bytes=VMEM_LIMIT),
        name="precondition",
    )(
        tiles,
        region,
        jnp.asarray(lanes_table(modes)),
        jnp.asarray(rows_table(modes)),
        jnp.asarray(columns_table(modes)),
        jnp.asarray(chebyshev_symbol()),
    )


def hamiltonian_tables():
    kinetic = -KINETIC_SCALE * circulant(kinetic_taps(), -14, GRID)
    magic = circulant(magic_taps(), -7, GRID)
    tables = (
        lanes_table_of_two(kinetic, magic),
        rows_table(kinetic),
        rows_table(magic),
        columns_table(kinetic),
        columns_table(magic),
        columns_table(magic.T),
        rows_table(magic.T),
        lanes_table(magic.T),
    )
    return [jnp.asarray(table) for table in tables]


def tile_of(index):
    return pl.ds(pl.multiple_of(index * 8, 8), 8)


def row_of(index):
    return pl.ds(index, 1)


TEAMS = 4
TEAM = DEVICES // TEAMS
LOGICAL = pl.DeviceIdType.LOGICAL
SEND_UNROLL = 8


def gradient_kernel(
    wave, potential_hbm, runs, lanes_kf, rows_k, rows_f, columns_k, columns_f, columns_b, rows_b, lanes_b,
    gradient_tiles, region_out,
    waves, staged, region, masked, kinetic, forward, potential,
    masked_send, masked_recv, applied_send, applied_recv, back_send,
    masked_split, partial, gathered, row, matrix,
    load_sems, send_sems, recv_sems,
):
    device = lax.axis_index("orb") * 2 + lax.axis_index("pair")
    my_team = jnp.bitwise_and(device, TEAMS - 1)
    my_seat = lax.shift_right_logical(device, 2)
    me = my_team * TEAM + my_seat
    barrier = pltpu.get_barrier_semaphore()

    def greet(step):
        peer = jnp.bitwise_and(device + (step + 1), DEVICES - 1)
        pl.semaphore_signal(barrier, inc=1, device_id=peer, device_id_type=LOGICAL)

    load_planes(wave.at[0], waves, load_sems.at[0])
    loop(DEVICES - 1, greet, SEND_UNROLL)
    load_planes(potential_hbm, staged, load_sems.at[1])
    bounds = run_bounds(runs[...])
    wait_planes(waves, load_sems.at[0])

    def team_after(stage):
        return jnp.bitwise_and(my_team + (stage + 1), TEAMS - 1)

    def team_before(stage):
        return jnp.bitwise_and(my_team + (TEAMS - 1 - stage), TEAMS - 1)

    def send_team(source, target, phase, team, count, source_at, target_at, signal):
        def send(step):
            seat = jnp.bitwise_and(my_seat + (step + 1), TEAM - 1)
            pltpu.make_async_remote_copy(
                src_ref=source.at[source_at(team * TEAM + seat)],
                dst_ref=target.at[target_at(me)],
                send_sem=send_sems.at[phase],
                recv_sem=recv_sems.at[phase, signal],
                device_id=seat * TEAMS + team,
                device_id_type=LOGICAL,
            ).start()

        loop(count, send, SEND_UNROLL)

    def size_of(stage):
        return TEAM if stage < TEAMS - 1 else TEAM - 1

    def scatter(source, target, phase, source_at, target_at, signal=0):
        for stage in range(TEAMS):
            send_team(
                source, target, phase, team_after(stage), size_of(stage), source_at, target_at, signal
            )

    def drain(buffer, sem, count=DEVICES - 1):
        whole = buffer.at[pl.ds(0, buffer.shape[0] * count // DEVICES)]
        pltpu.make_async_copy(whole, whole, sem).wait()

    def head(group):
        values = []
        for pair in pairs_of(group):
            mask = region_pair(bounds, pair)
            put_both_planes(region, pair, mask, block_of)
            value = both_planes(waves, pair, block_of) * mask
            put_both_planes(masked, pair, value)
            masked_send[block_of(pair), :] = fold_pair(value)
            values.append(value)
        hamiltonian_head(kinetic, forward, (lanes_kf, rows_k, rows_f), group, values)

    loop(GROUPS, head)
    region_copy = pltpu.make_async_copy(region, region_out, load_sems.at[2])
    region_copy.start()
    wait_planes(staged, load_sems.at[1])

    def pitch(pair):
        put_both_planes(potential, pair, both_planes(staged, pair, block_of))

    loop(PLANES // 2, pitch, 4)
    pl.semaphore_wait(barrier, DEVICES - 1)
    scatter(masked_send, masked_recv, 0, tile_of, tile_of)
    masked_recv[tile_of(me), :] = masked_send[tile_of(me), :]

    def middle(step):
        hamiltonian_middle(
            masked, kinetic, forward, potential, (columns_k, columns_f, columns_b), step
        )

    loop(GRID // 4, middle, MIDDLE_UNROLL)

    def tail(stage, count):
        team = team_after(stage)
        values = hamiltonian_tail(kinetic, forward, (rows_b, lanes_b), team)
        for pair, value in zip(pairs_of(team), values):
            applied_send[block_of(pair), :] = fold_pair(value * both_planes(region, pair, block_of))
        send_team(applied_send, applied_recv, 1, team, count, tile_of, tile_of, my_team)

    loop(TEAMS - 1, lambda stage: tail(stage, TEAM))
    tail(TEAMS - 1, TEAM - 1)
    applied_recv[tile_of(me), :] = applied_send[tile_of(me), :]
    drain(masked_recv, recv_sems.at[0, 0])
    for sub in range(8):
        high, low = split_pair(masked_recv[pl.ds(sub, DEVICES, stride=8), :])
        masked_split[:DEVICES, sub * 128 : sub * 128 + 128] = high
        masked_split[DEVICES:, sub * 128 : sub * 128 + 128] = low

    def strided(team, sub):
        return pl.ds(team * (TEAM * 8) + sub, TEAM, stride=8)

    def correlate(stage, count):
        team = team_before(stage)
        drain(applied_recv, recv_sems.at[1, team], count)
        parts = [split_pair(applied_recv[strided(team, sub), :]) for sub in range(8)]
        left = jnp.concatenate(
            [jnp.concatenate([part[which] for part in parts], axis=1) for which in range(2)], axis=0
        )
        total = lax.dot_general(
            left, masked_split[...], (((1,), (1,)), ((), ())), preferred_element_type=F32
        )
        rows = total[:TEAM, :DEVICES] + (total[:TEAM, DEVICES:] + total[TEAM:, :DEVICES])
        partial[pl.ds(team * TEAM, TEAM), 0, :] = rows
        send_team(partial, gathered, 2, team, count, row_of, row_of, 0)

    loop(TEAMS - 1, lambda stage: correlate(stage, TEAM))
    correlate(TEAMS - 1, TEAM - 1)
    gathered[row_of(me)] = partial[row_of(me)]
    drain(gathered, recv_sems.at[2, 0])
    row[...] = jnp.sum(gathered[...], axis=0, keepdims=True) * (1.0 / CELLS)
    scatter(row, matrix, 3, lambda peer: pl.ds(0, 1), row_of, my_team)
    matrix[row_of(me)] = row[...]

    def project(stage, count):
        team = team_before(stage)
        drain(matrix, recv_sems.at[3, team], count)
        high, low = split_pair(matrix[pl.ds(team * TEAM, TEAM), 0, :])
        table = jnp.concatenate([high, high, low], axis=1)
        for sub in range(0, 8, 2):
            lanes = slice(sub * 128, sub * 128 + 256)
            projected = dot32(
                table,
                jnp.concatenate([masked_split[:, lanes], masked_split[:DEVICES, lanes]], axis=0),
            )
            for shift in range(2):
                rows = strided(team, sub + shift)
                back_send[rows, :] = (
                    applied_recv[rows, :] - projected[:, shift * 128 : shift * 128 + 128]
                )
        send_team(back_send, gradient_tiles, 4, team, count, tile_of, tile_of, 0)

    loop(TEAMS - 1, lambda stage: project(stage, TEAM))
    project(TEAMS - 1, TEAM - 1)
    gradient_tiles[tile_of(me), :] = back_send[tile_of(me), :]
    region_copy.wait()
    drain(masked_send, send_sems.at[0])
    drain(applied_send, send_sems.at[1])
    drain(partial, send_sems.at[2])
    drain(matrix, send_sems.at[3])
    drain(gradient_tiles, recv_sems.at[4, 0])
    drain(back_send, send_sems.at[4])


def gradient_fields(wavefunctions, potential, line_runs):
    field = pltpu.VMEM(FIELD, F32)
    pitched = pltpu.VMEM(PITCHED, F32)
    tiles = pltpu.VMEM(TILES, F32)
    rows = pltpu.VMEM((DEVICES, 1, 128), F32)
    return pl.pallas_call(
        gradient_kernel,
        out_shape=(jax.ShapeDtypeStruct(TILES, F32), jax.ShapeDtypeStruct(FIELD, F32)),
        in_specs=anywhere(2) + in_vmem(9),
        out_specs=in_vmem(1) + anywhere(1),
        scratch_shapes=[
            field, field, field, pitched, pitched, pitched, pitched,
            tiles, tiles, tiles, tiles, tiles,
            pltpu.VMEM((2 * DEVICES, 8 * 128), BF16),
            rows, rows, pltpu.VMEM((1, 1, 128), F32), rows,
            pltpu.SemaphoreType.DMA((3,)),
            pltpu.SemaphoreType.DMA((5,)),
            pltpu.SemaphoreType.DMA((5, TEAMS)),
        ],
        compiler_params=pltpu.CompilerParams(
            collective_id=0, has_side_effects=True, vmem_limit_bytes=VMEM_LIMIT
        ),
        name="gradient",
    )(wavefunctions, potential, line_runs, *hamiltonian_tables())


def on_device(wavefunctions, potential, line_runs):
    tiles, region = gradient_fields(wavefunctions, potential, line_runs)
    return precondition(tiles, region)


def solution(mesh):
    return jax.shard_map(
        on_device,
        mesh=mesh,
        in_specs=(P(("orb", "pair"), None, None), P(), P()),
        out_specs=(P(("orb", "pair"), None, None), P(("orb", "pair"), None, None)),
        check_vma=False,
    )
```

```python
import math

import jax
import jax.numpy as jnp
import numpy as np
from jax import lax
from jax.experimental import pallas as pl
from jax.experimental.pallas import tpu as pltpu
from jax.sharding import PartitionSpec as P

GRID = 64
CHEB = 6
CELLS = GRID * GRID * GRID
PLANES = GRID // 2
DEVICES = 128
KINETIC_SCALE = 0.125
SHIFT_VALUE = 0.25
VMEM_LIMIT = 56 * 1024 * 1024
BF16 = jnp.bfloat16
F32 = jnp.float32


def kinetic_taps():
    radius = 14
    values = np.zeros(2 * radius + 1)
    factor = float(math.factorial(radius)) ** 2
    for offset in range(1, radius + 1):
        weight = (
            2.0
            * (-1.0) ** (offset + 1)
            * factor
            / (
                offset
                * offset
                * float(math.factorial(radius - offset))
                * float(math.factorial(radius + offset))
            )
        )
        values[radius + offset] = weight
        values[radius - offset] = weight
    values[radius] = -2.0 * sum((1.0 / float(offset * offset) for offset in range(1, radius + 1)))
    return values


def magic_taps():
    shifted = np.arange(-7, 9) - 0.25
    sinc_values = np.sin(np.pi * shifted) / (np.pi * shifted)
    values = sinc_values * (0.5 + 0.5 * np.cos(np.pi * shifted / 8.5))
    return values / values.sum()


def circulant(values, first, length):
    matrix = np.zeros((length, length))
    for target in range(length):
        for position in range(values.shape[0]):
            matrix[target, (target + first + position) % length] += values[position]
    return matrix


def kinetic_spectrum():
    taps = -KINETIC_SCALE * kinetic_taps()
    offsets = np.arange(-14, 15)
    modes = np.arange(GRID).reshape(GRID, 1)
    return np.cos(2.0 * np.pi * modes * offsets.reshape(1, -1) / GRID) @ taps


def hartley():
    angle = 2.0 * np.pi * np.outer(np.arange(GRID), np.arange(GRID)) / GRID
    return (np.cos(angle) + np.sin(angle)) / np.sqrt(GRID)


def chebyshev_symbol():
    line = kinetic_spectrum()
    low_end = SHIFT_VALUE
    high_end = SHIFT_VALUE + 3.0 * float(line.max())
    centre_value = 0.5 * (high_end + low_end)
    half_width = 0.5 * (high_end - low_end)
    ratio_base = centre_value / half_width
    rho_value = 1.0 / ratio_base
    operator = line[:, None, None] + line[None, :, None] + line[None, None, :] + SHIFT_VALUE
    solution_value = np.zeros_like(operator)
    residual = np.ones_like(operator)
    direction = residual / centre_value
    for counter in range(CHEB):
        solution_value = solution_value + direction
        if counter + 1 < CHEB:
            residual = residual - operator * direction
            rho_next = 1.0 / (2.0 * ratio_base - rho_value)
            direction = rho_next * rho_value * direction + 2.0 * rho_next / half_width * residual
            rho_value = rho_next
    blocks = solution_value.reshape(GRID // 4, 2, 2, PLANES, 2, GRID)
    return blocks.transpose(0, 4, 3, 1, 2, 5).reshape(GRID // 4 * GRID, 256).astype(np.float32)


def split_table(matrix):
    high = np.asarray(matrix, np.float32).astype(jnp.bfloat16)
    low = (np.asarray(matrix, np.float64) - high.astype(np.float64)).astype(np.float32).astype(jnp.bfloat16)
    return high, low


def rows_table(matrix):
    high, low = split_table(matrix)
    return np.concatenate([high, high, low], axis=1)


def columns_table(matrix):
    order = np.concatenate([np.arange(0, GRID, 2), np.arange(1, GRID, 2)])
    return rows_table(matrix[order][:, order])


def lanes_table(matrix):
    high, low = split_table(np.kron(np.eye(2), matrix.T))
    both = np.concatenate([high, low], axis=1)
    return np.concatenate([both, both], axis=0)


def lanes_table_of_two(first, second):
    parts = [split_table(np.kron(np.eye(2), matrix.T)) for matrix in (first, second)]
    high = np.concatenate([part[0] for part in parts], axis=1)
    low = np.concatenate([part[1] for part in parts], axis=1)
    return np.concatenate([high, high, low], axis=0)


def split_pair(value):
    high = value.astype(BF16)
    low = (value - high.astype(F32)).astype(BF16)
    return high, low


def dot32(left, right):
    return jnp.dot(left, right, preferred_element_type=F32)


def along_rows(table, value):
    high, low = split_pair(value)
    return dot32(table, jnp.concatenate([high, low, high], axis=0))


def along_lanes(table, value):
    high, low = split_pair(value)
    product = dot32(jnp.concatenate([high, low], axis=1), table)
    return product[:, :128] + product[:, 128:]


def along_lanes_of_two(table, value):
    high, low = split_pair(value)
    product = dot32(jnp.concatenate([high, low, high], axis=1), table)
    return product[:, :128], product[:, 128:]


def lane_index(shape):
    return lax.broadcasted_iota(jnp.int32, shape, 1)


PITCH = GRID + 1
PITCHED = (PITCH * PLANES, 128)


def x_rows(first):
    return pl.ds(first, PLANES, stride=PITCH)


def turn(first, second):
    half = lane_index((PLANES, 128)) < 64
    return (
        jnp.where(half, first, pltpu.roll(second, 64, 1)),
        jnp.where(half, pltpu.roll(first, 64, 1), second),
    )


def columns_of(ref, first):
    pairs = [
        jnp.concatenate(turn(ref[x_rows(first + shift), :], ref[x_rows(first + shift + 1), :]), axis=0)
        for shift in (0, 2)
    ]
    return jnp.concatenate(pairs, axis=1)


def x_planes(value):
    return (
        *turn(value[:PLANES, :128], value[PLANES:, :128]),
        *turn(value[:PLANES, 128:], value[PLANES:, 128:]),
    )


def put_columns(ref, first, value):
    for shift, plane in enumerate(x_planes(value)):
        ref[x_rows(first + shift), :] = plane


def add_columns(ref, first, value):
    for shift, plane in enumerate(x_planes(value)):
        ref[x_rows(first + shift), :] = ref[x_rows(first + shift), :] + plane


def block_of(plane):
    return pl.ds(pl.multiple_of(plane * GRID, GRID), GRID)


def run_bounds(runs):
    row = lax.broadcasted_iota(jnp.int32, (GRID, PLANES), 0)
    column = lax.broadcasted_iota(jnp.int32, (GRID, PLANES), 1)
    repeat = (row // 2 == column).astype(F32).astype(BF16)
    own = lax.broadcasted_iota(jnp.int32, (GRID, 128), 0) % 2 == lane_index((GRID, 128)) // 64
    bounds = []
    for bound in range(2):
        lines = runs[bound : bound + 1, :].reshape(PLANES, 128).astype(F32).astype(BF16)
        bounds.append(jnp.where(own, dot32(repeat, lines), 0.0))
    return jnp.concatenate(bounds, axis=0).astype(BF16)


def region_pair(bounds, pair):
    lane = lane_index((128, 256))
    line = lax.broadcasted_iota(jnp.int32, (128, 256), 0) % GRID
    pick = (line == lane // 64 + 4 * pair).astype(F32).astype(BF16)
    spread = dot32(bounds, pick)
    depth = (lane_index((GRID, 256)) % GRID).astype(F32)
    return ((depth >= spread[:GRID]) & (depth < spread[GRID:])).astype(F32)


def fold_pair(value):
    first, second = value[:, :128], value[:, 128:]
    lower = (lane_index((GRID, 128)) // 32) % 2 == 0
    return jnp.where(lower, first + pltpu.roll(first, 96, 1), second + pltpu.roll(second, 32, 1))


def unfold_pair(tile):
    lower = (lane_index((GRID, 128)) // 32) % 2 == 0
    first = jnp.where(lower, tile, pltpu.roll(tile, 32, 1))
    second = jnp.where(lower, pltpu.roll(tile, 96, 1), tile)
    return jnp.concatenate([first, second], axis=1)


def load_planes(hbm, vmem, sem):
    for plane in range(PLANES):
        pltpu.make_async_copy(
            hbm.at[:, pl.ds(plane * 128, 128)], vmem.at[pl.ds(plane * GRID, GRID), :], sem
        ).start()


def wait_planes(vmem, sem):
    pltpu.make_async_copy(vmem, vmem, sem).wait()


def pitched_block(plane):
    return pl.ds(plane * PITCH, GRID)


def both_planes(ref, pair, at=pitched_block):
    return jnp.concatenate([ref[at(2 * pair), :], ref[at(2 * pair + 1), :]], axis=1)


def put_both_planes(ref, pair, value, at=pitched_block):
    ref[at(2 * pair), :] = value[:, :128]
    ref[at(2 * pair + 1), :] = value[:, 128:]


def stacked(values):
    return jnp.concatenate([half for value in values for half in (value[:, :128], value[:, 128:])], axis=0)


def unstacked(value):
    return [
        jnp.concatenate([value[row : row + GRID], value[row + GRID : row + 2 * GRID]], axis=1)
        for row in range(0, value.shape[0], 2 * GRID)
    ]


GROUP = 4
GROUPS = PLANES // 2 // GROUP


def pairs_of(group):
    return [group * GROUP + member for member in range(GROUP)]


def hamiltonian_head(kinetic, forward, tables, group, values):
    lanes_kf, rows_k, rows_f = tables
    along, magic = along_lanes_of_two(lanes_kf[...], stacked(values))
    for pair, value, first, second in zip(pairs_of(group), values, unstacked(along), unstacked(magic)):
        put_both_planes(kinetic, pair, first + along_rows(rows_k[...], value))
        put_both_planes(forward, pair, along_rows(rows_f[...], second))


def hamiltonian_middle(masked, kinetic, forward, potential, tables, step):
    columns_k, columns_f, columns_b = tables
    first = 4 * step
    real = along_rows(columns_f[...], columns_of(forward, first))
    weighted = real * columns_of(potential, first)
    put_columns(forward, first, along_rows(columns_b[...], weighted))
    add_columns(kinetic, first, along_rows(columns_k[...], columns_of(masked, first)))


def hamiltonian_tail(kinetic, forward, tables, group):
    rows_b, lanes_b = tables
    values = [along_rows(rows_b[...], both_planes(forward, pair)) for pair in pairs_of(group)]
    returned = unstacked(along_lanes(lanes_b[...], stacked(values)))
    return [both_planes(kinetic, pair) + value for pair, value in zip(pairs_of(group), returned)]


def loop(count, body, unroll=1):
    def step(index, carry):
        body(index)
        return carry

    lax.fori_loop(0, count, step, 0, unroll=unroll)


def precondition_kernel(
    tiles_hbm, region_hbm, lanes_q, rows_q, columns_q, symbol_hbm, gradient_out, preconditioned_out,
    tiles, region, gradient, work, symbol, load_sems, sems,
):
    def fetch(group):
        rows = pl.ds(group * GROUP * GRID, GROUP * GRID)
        planes = pl.ds(group * GROUP * 2 * GRID, GROUP * 2 * GRID)
        return (
            pltpu.make_async_copy(tiles_hbm.at[rows], tiles.at[rows], load_sems.at[0, group]),
            pltpu.make_async_copy(region_hbm.at[planes], region.at[planes], load_sems.at[1, group]),
        )

    for group in range(GROUPS):
        for copy in fetch(group):
            copy.start()
    symbol_copy = pltpu.make_async_copy(symbol_hbm, symbol, sems.at[0])
    symbol_copy.start()

    def put(buffer, target, pair, sem):
        for plane in (2 * pair, 2 * pair + 1):
            pltpu.make_async_copy(
                buffer.at[block_of(plane), :],
                target.at[0, :, pl.ds(pl.multiple_of(plane * 128, 128), 128)],
                sem,
            ).start()

    def head(group):
        for copy in fetch(group):
            copy.wait()
        values = []
        for pair in pairs_of(group):
            value = unfold_pair(tiles[block_of(pair), :]) * both_planes(region, pair, block_of)
            put_both_planes(gradient, pair, value, block_of)
            put(gradient, gradient_out, pair, sems.at[1])
            values.append(value)
        turned = unstacked(along_lanes(lanes_q[...], stacked(values)))
        for pair, value in zip(pairs_of(group), turned):
            put_both_planes(work, pair, along_rows(rows_q[...], value))

    loop(GROUPS, head, GROUPS)
    symbol_copy.wait()

    def middle(step):
        first = 4 * step
        modes = along_rows(columns_q[...], columns_of(work, first)) * symbol[block_of(step), :]
        put_columns(work, first, along_rows(columns_q[...], modes))

    loop(GRID // 4, middle, MIDDLE_UNROLL)
    wait_planes(gradient, sems.at[1])

    def tail(group):
        values = [along_rows(rows_q[...], both_planes(work, pair)) for pair in pairs_of(group)]
        turned = unstacked(along_lanes(lanes_q[...], stacked(values)))
        for pair, value in zip(pairs_of(group), turned):
            put_both_planes(gradient, pair, value * both_planes(region, pair, block_of), block_of)
            put(gradient, preconditioned_out, pair, sems.at[2])

    loop(GROUPS, tail, GROUPS)
    wait_planes(gradient, sems.at[2])


MIDDLE_UNROLL = GRID // 4


def in_vmem(count):
    return [pl.BlockSpec(memory_space=pltpu.VMEM)] * count


def anywhere(count):
    return [pl.BlockSpec(memory_space=pl.ANY)] * count


FIELD = (GRID * PLANES, 128)
TILES = (8 * DEVICES, 128)


def precondition(tiles, region):
    modes = hartley()
    field = pltpu.VMEM(FIELD, F32)
    pitched = pltpu.VMEM(PITCHED, F32)
    shape = jax.ShapeDtypeStruct((1, GRID, GRID * GRID), F32)
    return pl.pallas_call(
        precondition_kernel,
        out_shape=(shape, shape),
        in_specs=anywhere(2) + in_vmem(3) + anywhere(1),
        out_specs=anywhere(2),
        scratch_shapes=[
            pltpu.VMEM(TILES, F32), field, field, pitched, pltpu.VMEM((GRID // 4 * GRID, 256), F32),
            pltpu.SemaphoreType.DMA((2, GROUPS)),
            pltpu.SemaphoreType.DMA((3,)),
        ],
        compiler_params=pltpu.CompilerParams(vmem_limit_bytes=VMEM_LIMIT),
        name="precondition",
    )(
        tiles,
        region,
        jnp.asarray(lanes_table(modes)),
        jnp.asarray(rows_table(modes)),
        jnp.asarray(columns_table(modes)),
        jnp.asarray(chebyshev_symbol()),
    )


def hamiltonian_tables():
    kinetic = -KINETIC_SCALE * circulant(kinetic_taps(), -14, GRID)
    magic = circulant(magic_taps(), -7, GRID)
    tables = (
        lanes_table_of_two(kinetic, magic),
        rows_table(kinetic),
        rows_table(magic),
        columns_table(kinetic),
        columns_table(magic),
        columns_table(magic.T),
        rows_table(magic.T),
        lanes_table(magic.T),
    )
    return [jnp.asarray(table) for table in tables]


def tile_of(index):
    return pl.ds(pl.multiple_of(index * BLOCK, BLOCK), BLOCK)


def row_of(index):
    return pl.ds(index, 1)


TEAMS = 4
CHIPS = DEVICES // 2
TEAM = CHIPS // TEAMS
BLOCK = 16
LOGICAL = pl.DeviceIdType.LOGICAL
SEND_UNROLL = 8


def gradient_kernel(
    wave, potential_hbm, runs, lanes_kf, rows_k, rows_f, columns_k, columns_f, columns_b, rows_b, lanes_b,
    gradient_tiles, region_out,
    waves, staged, region, masked, kinetic, forward, potential,
    masked_send, masked_recv, applied_send, applied_recv, back_send,
    masked_split, partial, gathered, row, matrix,
    load_sems, send_sems, recv_sems,
):
    chip = lax.axis_index("orb")
    core = lax.axis_index("pair")
    my_team = jnp.bitwise_and(lax.shift_right_logical(chip, 1), 2) + jnp.bitwise_and(chip, 1)
    my_seat = jnp.bitwise_and(lax.shift_right_logical(chip, 2), 14) + jnp.bitwise_and(
        lax.shift_right_logical(chip, 1), 1
    )
    me = my_team * TEAM + my_seat
    my_half = core * CHIPS
    barrier = pltpu.get_barrier_semaphore()

    def greet(step):
        peer = jnp.bitwise_and(chip + (step + 1), CHIPS - 1) * 2 + core
        pl.semaphore_signal(barrier, inc=1, device_id=peer, device_id_type=LOGICAL)

    load_planes(wave.at[0], waves, load_sems.at[0])
    loop(CHIPS - 1, greet, SEND_UNROLL)
    partner = chip * 2 + (1 - core)
    pl.semaphore_signal(barrier, inc=1, device_id=partner, device_id_type=LOGICAL)
    load_planes(potential_hbm, staged, load_sems.at[1])
    bounds = run_bounds(runs[...])
    wait_planes(waves, load_sems.at[0])

    def team_after(stage):
        return jnp.bitwise_and(my_team + (stage + 1), TEAMS - 1)

    def team_before(stage):
        return jnp.bitwise_and(my_team + (TEAMS - 1 - stage), TEAMS - 1)

    def send_team(source, target, phase, team, count, source_at, target_at, signal):
        base = jnp.bitwise_and(team, 2) * 4 + jnp.bitwise_and(team, 1) * 2 + core

        def send(step):
            seat = jnp.bitwise_and(my_seat + (step + 1), TEAM - 1)
            pltpu.make_async_remote_copy(
                src_ref=source.at[source_at(team * TEAM + seat)],
                dst_ref=target.at[target_at(me)],
                send_sem=send_sems.at[phase],
                recv_sem=recv_sems.at[phase, signal],
                device_id=jnp.bitwise_and(seat, 14) * 8 + jnp.bitwise_and(seat, 1) * 4 + base,
                device_id_type=LOGICAL,
            ).start()

        loop(count, send, SEND_UNROLL)

    def size_of(stage):
        return TEAM if stage < TEAMS - 1 else TEAM - 1

    def scatter(source, target, phase, source_at, target_at, signal=0):
        for stage in range(TEAMS):
            send_team(
                source, target, phase, team_after(stage), size_of(stage), source_at, target_at, signal
            )

    def drain(buffer, sem, count=CHIPS - 1):
        whole = buffer.at[pl.ds(0, buffer.shape[0] * count // CHIPS)]
        pltpu.make_async_copy(whole, whole, sem).wait()

    def head(group):
        values = []
        for pair in pairs_of(group):
            mask = region_pair(bounds, pair)
            put_both_planes(region, pair, mask, block_of)
            value = both_planes(waves, pair, block_of) * mask
            put_both_planes(masked, pair, value)
            masked_send[block_of(pair), :] = fold_pair(value)
            values.append(value)
        hamiltonian_head(kinetic, forward, (lanes_kf, rows_k, rows_f), group, values)

    loop(GROUPS, head, GROUPS)
    region_copy = pltpu.make_async_copy(region, region_out, load_sems.at[2])
    region_copy.start()
    wait_planes(staged, load_sems.at[1])

    def pitch(pair):
        put_both_planes(potential, pair, both_planes(staged, pair, block_of))

    loop(PLANES // 2, pitch, 4)
    pl.semaphore_wait(barrier, CHIPS)
    scatter(masked_send, masked_recv, 0, tile_of, lambda label: tile_of(my_half + label))
    masked_recv[tile_of(my_half + me), :] = masked_send[tile_of(me), :]

    def middle(step):
        hamiltonian_middle(
            masked, kinetic, forward, potential, (columns_k, columns_f, columns_b), step
        )

    loop(GRID // 4, middle, MIDDLE_UNROLL)

    def tail(stage, count):
        team = team_after(stage)
        values = hamiltonian_tail(kinetic, forward, (rows_b, lanes_b), team)
        for pair, value in zip(pairs_of(team), values):
            applied_send[block_of(pair), :] = fold_pair(value * both_planes(region, pair, block_of))
        send_team(applied_send, applied_recv, 1, team, count, tile_of, tile_of, my_team)

    loop(TEAMS - 1, lambda stage: tail(stage, TEAM))
    tail(TEAMS - 1, TEAM - 1)
    applied_recv[tile_of(me), :] = applied_send[tile_of(me), :]
    drain(masked_recv.at[pl.ds(0, CHIPS * BLOCK)], recv_sems.at[0, 0])
    kind = masked_recv.at[pl.ds(pl.multiple_of(my_half * BLOCK, BLOCK), CHIPS * BLOCK), :]
    swap = pltpu.make_async_remote_copy(
        src_ref=kind, dst_ref=kind, send_sem=send_sems.at[5], recv_sem=recv_sems.at[5, 0],
        device_id=partner, device_id_type=LOGICAL,
    )
    swap.start()

    def split_half(first):
        for sub in range(BLOCK):
            rows = pl.ds(first * BLOCK + sub, CHIPS, stride=BLOCK)
            high, low = split_pair(masked_recv[rows, :])
            lanes = slice(sub * 128, sub * 128 + 128)
            masked_split[pl.ds(pl.multiple_of(first, CHIPS), CHIPS), lanes] = high
            masked_split[pl.ds(pl.multiple_of(first, CHIPS) + DEVICES, CHIPS), lanes] = low

    split_half(my_half)
    swap.wait()
    split_half(CHIPS - my_half)

    def strided(team, sub):
        return pl.ds(team * (TEAM * BLOCK) + sub, TEAM, stride=BLOCK)

    def correlate(stage, count):
        team = team_before(stage)
        drain(applied_recv, recv_sems.at[1, team], count)
        parts = [split_pair(applied_recv[strided(team, sub), :]) for sub in range(BLOCK)]
        left = jnp.concatenate(
            [jnp.concatenate([part[which] for part in parts], axis=1) for which in range(2)], axis=0
        )
        total = lax.dot_general(
            left, masked_split[...], (((1,), (1,)), ((), ())), preferred_element_type=F32
        )
        rows = total[:TEAM, :DEVICES] + (total[:TEAM, DEVICES:] + total[TEAM:, :DEVICES])
        partial[pl.ds(team * TEAM, TEAM), 0, :] = rows
        send_team(partial, gathered, 2, team, count, row_of, row_of, 0)

    loop(TEAMS - 1, lambda stage: correlate(stage, TEAM))
    correlate(TEAMS - 1, TEAM - 1)
    gathered[row_of(me)] = partial[row_of(me)]
    drain(gathered, recv_sems.at[2, 0])
    row[...] = jnp.sum(gathered[...], axis=0, keepdims=True) * (1.0 / CELLS)
    scatter(row, matrix, 3, lambda peer: pl.ds(0, 1), row_of, my_team)
    matrix[row_of(me)] = row[...]

    def project(stage, count):
        team = team_before(stage)
        drain(matrix, recv_sems.at[3, team], count)
        high, low = split_pair(matrix[pl.ds(team * TEAM, TEAM), 0, :])
        table = jnp.concatenate([high, high, low], axis=1)
        for sub in range(0, BLOCK, 2):
            lanes = slice(sub * 128, sub * 128 + 256)
            projected = dot32(
                table,
                jnp.concatenate([masked_split[:, lanes], masked_split[:DEVICES, lanes]], axis=0),
            )
            for shift in range(2):
                rows = strided(team, sub + shift)
                back_send[rows, :] = (
                    applied_recv[rows, :] - projected[:, shift * 128 : shift * 128 + 128]
                )
        send_team(back_send, gradient_tiles, 4, team, count, tile_of, tile_of, 0)

    loop(TEAMS - 1, lambda stage: project(stage, TEAM))
    project(TEAMS - 1, TEAM - 1)
    gradient_tiles[tile_of(me), :] = back_send[tile_of(me), :]
    region_copy.wait()
    drain(masked_send, send_sems.at[0])
    drain(applied_send, send_sems.at[1])
    drain(partial, send_sems.at[2])
    drain(matrix, send_sems.at[3])
    drain(gradient_tiles, recv_sems.at[4, 0])
    drain(back_send, send_sems.at[4])


def gradient_fields(wavefunctions, potential, line_runs):
    field = pltpu.VMEM(FIELD, F32)
    pitched = pltpu.VMEM(PITCHED, F32)
    tiles = pltpu.VMEM(TILES, F32)
    rows = pltpu.VMEM((CHIPS, 1, 128), F32)
    return pl.pallas_call(
        gradient_kernel,
        out_shape=(jax.ShapeDtypeStruct(TILES, F32), jax.ShapeDtypeStruct(FIELD, F32)),
        in_specs=anywhere(2) + in_vmem(9),
        out_specs=in_vmem(1) + anywhere(1),
        scratch_shapes=[
            field, field, field, pitched, pitched, pitched, pitched,
            tiles, pltpu.VMEM((2 * TILES[0], 128), F32), tiles, tiles, tiles,
            pltpu.VMEM((2 * DEVICES, BLOCK * 128), BF16),
            rows, rows, pltpu.VMEM((1, 1, 128), F32), rows,
            pltpu.SemaphoreType.DMA((3,)),
            pltpu.SemaphoreType.DMA((6,)),
            pltpu.SemaphoreType.DMA((6, TEAMS)),
        ],
        compiler_params=pltpu.CompilerParams(
            collective_id=0, has_side_effects=True, vmem_limit_bytes=VMEM_LIMIT
        ),
        name="gradient",
    )(wavefunctions, potential, line_runs, *hamiltonian_tables())


def on_device(wavefunctions, potential, line_runs):
    tiles, region = gradient_fields(wavefunctions, potential, line_runs)
    return precondition(tiles, region)


def solution(mesh):
    return jax.shard_map(
        on_device,
        mesh=mesh,
        in_specs=(P(("orb", "pair"), None, None), P(), P()),
        out_specs=(P(("orb", "pair"), None, None), P(("orb", "pair"), None, None)),
        check_vma=False,
    )
```

```python
import math

import jax
import jax.numpy as jnp
import numpy as np
from jax import lax
from jax.experimental import pallas as pl
from jax.experimental.pallas import tpu as pltpu
from jax.sharding import PartitionSpec as P

GRID = 64
CHEB = 6
CELLS = GRID * GRID * GRID
PLANES = GRID // 2
DEVICES = 128
KINETIC_SCALE = 0.125
SHIFT_VALUE = 0.25
VMEM_LIMIT = 56 * 1024 * 1024
BF16 = jnp.bfloat16
F32 = jnp.float32


def kinetic_taps():
    radius = 14
    values = np.zeros(2 * radius + 1)
    factor = float(math.factorial(radius)) ** 2
    for offset in range(1, radius + 1):
        weight = (
            2.0
            * (-1.0) ** (offset + 1)
            * factor
            / (
                offset
                * offset
                * float(math.factorial(radius - offset))
                * float(math.factorial(radius + offset))
            )
        )
        values[radius + offset] = weight
        values[radius - offset] = weight
    values[radius] = -2.0 * sum((1.0 / float(offset * offset) for offset in range(1, radius + 1)))
    return values


def magic_taps():
    shifted = np.arange(-7, 9) - 0.25
    sinc_values = np.sin(np.pi * shifted) / (np.pi * shifted)
    values = sinc_values * (0.5 + 0.5 * np.cos(np.pi * shifted / 8.5))
    return values / values.sum()


def circulant(values, first, length):
    matrix = np.zeros((length, length))
    for target in range(length):
        for position in range(values.shape[0]):
            matrix[target, (target + first + position) % length] += values[position]
    return matrix


def kinetic_spectrum():
    taps = -KINETIC_SCALE * kinetic_taps()
    offsets = np.arange(-14, 15)
    modes = np.arange(GRID).reshape(GRID, 1)
    return np.cos(2.0 * np.pi * modes * offsets.reshape(1, -1) / GRID) @ taps


def hartley():
    angle = 2.0 * np.pi * np.outer(np.arange(GRID), np.arange(GRID)) / GRID
    return (np.cos(angle) + np.sin(angle)) / np.sqrt(GRID)


def chebyshev_symbol():
    line = kinetic_spectrum()
    low_end = SHIFT_VALUE
    high_end = SHIFT_VALUE + 3.0 * float(line.max())
    centre_value = 0.5 * (high_end + low_end)
    half_width = 0.5 * (high_end - low_end)
    ratio_base = centre_value / half_width
    rho_value = 1.0 / ratio_base
    operator = line[:, None, None] + line[None, :, None] + line[None, None, :] + SHIFT_VALUE
    solution_value = np.zeros_like(operator)
    residual = np.ones_like(operator)
    direction = residual / centre_value
    for counter in range(CHEB):
        solution_value = solution_value + direction
        if counter + 1 < CHEB:
            residual = residual - operator * direction
            rho_next = 1.0 / (2.0 * ratio_base - rho_value)
            direction = rho_next * rho_value * direction + 2.0 * rho_next / half_width * residual
            rho_value = rho_next
    blocks = solution_value.reshape(GRID // 4, 2, 2, PLANES, 2, GRID)
    return blocks.transpose(0, 4, 3, 1, 2, 5).reshape(GRID // 4 * GRID, 256).astype(np.float32)


def split_table(matrix):
    high = np.asarray(matrix, np.float32).astype(jnp.bfloat16)
    low = (np.asarray(matrix, np.float64) - high.astype(np.float64)).astype(np.float32).astype(jnp.bfloat16)
    return high, low


def rows_table(matrix):
    high, low = split_table(matrix)
    return np.concatenate([high, high, low], axis=1)


def columns_table(matrix):
    order = np.concatenate([np.arange(0, GRID, 2), np.arange(1, GRID, 2)])
    return rows_table(matrix[order][:, order])


def lanes_table(matrix):
    high, low = split_table(np.kron(np.eye(2), matrix.T))
    both = np.concatenate([high, low], axis=1)
    return np.concatenate([both, both], axis=0)


def lanes_table_of_two(first, second):
    parts = [split_table(np.kron(np.eye(2), matrix.T)) for matrix in (first, second)]
    high = np.concatenate([part[0] for part in parts], axis=1)
    low = np.concatenate([part[1] for part in parts], axis=1)
    return np.concatenate([high, high, low], axis=0)


def split_pair(value):
    high = value.astype(BF16)
    low = (value - high.astype(F32)).astype(BF16)
    return high, low


def dot32(left, right):
    return jnp.dot(left, right, preferred_element_type=F32)


def along_rows(table, value):
    high, low = split_pair(value)
    return dot32(table, jnp.concatenate([high, low, high], axis=0))


def along_lanes(table, value):
    high, low = split_pair(value)
    product = dot32(jnp.concatenate([high, low], axis=1), table)
    return product[:, :128] + product[:, 128:]


def along_lanes_of_two(table, value):
    high, low = split_pair(value)
    product = dot32(jnp.concatenate([high, low, high], axis=1), table)
    return product[:, :128], product[:, 128:]


def lane_index(shape):
    return lax.broadcasted_iota(jnp.int32, shape, 1)


PITCH = GRID + 1
PITCHED = (PITCH * PLANES, 128)


def x_rows(first):
    return pl.ds(first, PLANES, stride=PITCH)


def turn(first, second):
    half = lane_index((PLANES, 128)) < 64
    return (
        jnp.where(half, first, pltpu.roll(second, 64, 1)),
        jnp.where(half, pltpu.roll(first, 64, 1), second),
    )


def columns_of(ref, first):
    pairs = [
        jnp.concatenate(turn(ref[x_rows(first + shift), :], ref[x_rows(first + shift + 1), :]), axis=0)
        for shift in (0, 2)
    ]
    return jnp.concatenate(pairs, axis=1)


def x_planes(value):
    return (
        *turn(value[:PLANES, :128], value[PLANES:, :128]),
        *turn(value[:PLANES, 128:], value[PLANES:, 128:]),
    )


def put_columns(ref, first, value):
    for shift, plane in enumerate(x_planes(value)):
        ref[x_rows(first + shift), :] = plane


def add_columns(ref, first, value):
    for shift, plane in enumerate(x_planes(value)):
        ref[x_rows(first + shift), :] = ref[x_rows(first + shift), :] + plane


def block_of(plane):
    return pl.ds(pl.multiple_of(plane * GRID, GRID), GRID)


def run_bounds(runs):
    row = lax.broadcasted_iota(jnp.int32, (GRID, PLANES), 0)
    column = lax.broadcasted_iota(jnp.int32, (GRID, PLANES), 1)
    repeat = (row // 2 == column).astype(F32).astype(BF16)
    own = lax.broadcasted_iota(jnp.int32, (GRID, 128), 0) % 2 == lane_index((GRID, 128)) // 64
    bounds = []
    for bound in range(2):
        lines = runs[bound : bound + 1, :].reshape(PLANES, 128).astype(F32).astype(BF16)
        bounds.append(jnp.where(own, dot32(repeat, lines), 0.0))
    return jnp.concatenate(bounds, axis=0).astype(BF16)


def region_pair(bounds, pair):
    lane = lane_index((128, 256))
    line = lax.broadcasted_iota(jnp.int32, (128, 256), 0) % GRID
    pick = (line == lane // 64 + 4 * pair).astype(F32).astype(BF16)
    spread = dot32(bounds, pick)
    depth = (lane_index((GRID, 256)) % GRID).astype(F32)
    return ((depth >= spread[:GRID]) & (depth < spread[GRID:])).astype(F32)


def fold_pair(value):
    first, second = value[:, :128], value[:, 128:]
    lower = (lane_index((GRID, 128)) // 32) % 2 == 0
    return jnp.where(lower, first + pltpu.roll(first, 96, 1), second + pltpu.roll(second, 32, 1))


def unfold_pair(tile):
    lower = (lane_index((GRID, 128)) // 32) % 2 == 0
    first = jnp.where(lower, tile, pltpu.roll(tile, 32, 1))
    second = jnp.where(lower, pltpu.roll(tile, 96, 1), tile)
    return jnp.concatenate([first, second], axis=1)


def load_planes(hbm, vmem, sem):
    for plane in range(PLANES):
        pltpu.make_async_copy(
            hbm.at[:, pl.ds(plane * 128, 128)], vmem.at[pl.ds(plane * GRID, GRID), :], sem
        ).start()


def wait_planes(vmem, sem):
    pltpu.make_async_copy(vmem, vmem, sem).wait()


def pitched_block(plane):
    return pl.ds(plane * PITCH, GRID)


def both_planes(ref, pair, at=pitched_block):
    return jnp.concatenate([ref[at(2 * pair), :], ref[at(2 * pair + 1), :]], axis=1)


def put_both_planes(ref, pair, value, at=pitched_block):
    ref[at(2 * pair), :] = value[:, :128]
    ref[at(2 * pair + 1), :] = value[:, 128:]


def stacked(values):
    return jnp.concatenate([half for value in values for half in (value[:, :128], value[:, 128:])], axis=0)


def unstacked(value):
    return [
        jnp.concatenate([value[row : row + GRID], value[row + GRID : row + 2 * GRID]], axis=1)
        for row in range(0, value.shape[0], 2 * GRID)
    ]


GROUP = 4
GROUPS = PLANES // 2 // GROUP


def pairs_of(group):
    return [group * GROUP + member for member in range(GROUP)]


def hamiltonian_head(kinetic, forward, tables, group, values):
    lanes_kf, rows_k, rows_f = tables
    along, magic = along_lanes_of_two(lanes_kf[...], stacked(values))
    for pair, value, first, second in zip(pairs_of(group), values, unstacked(along), unstacked(magic)):
        put_both_planes(kinetic, pair, first + along_rows(rows_k[...], value))
        put_both_planes(forward, pair, along_rows(rows_f[...], second))


def hamiltonian_middle(masked, kinetic, forward, potential, tables, step):
    columns_k, columns_f, columns_b = tables
    first = 4 * step
    real = along_rows(columns_f[...], columns_of(forward, first))
    weighted = real * columns_of(potential, first)
    put_columns(forward, first, along_rows(columns_b[...], weighted))
    add_columns(kinetic, first, along_rows(columns_k[...], columns_of(masked, first)))


def hamiltonian_tail(kinetic, forward, tables, group):
    rows_b, lanes_b = tables
    values = [along_rows(rows_b[...], both_planes(forward, pair)) for pair in pairs_of(group)]
    returned = unstacked(along_lanes(lanes_b[...], stacked(values)))
    return [both_planes(kinetic, pair) + value for pair, value in zip(pairs_of(group), returned)]


def loop(count, body, unroll=1):
    def step(index, carry):
        body(index)
        return carry

    lax.fori_loop(0, count, step, 0, unroll=unroll)


def copies_of(sources, targets, sems):
    return [
        pltpu.make_async_copy(source, target, sems.at[place])
        for place, (source, target) in enumerate(zip(sources, targets))
    ]


def precondition_kernel(
    tiles_hbm, region_hbm, lanes_hbm, rows_hbm, columns_hbm, symbol_hbm, gradient_out, preconditioned_out,
    lanes_q, rows_q, columns_q, symbol, tiles, region, gradient, work, table_sems, load_sems, sems,
):
    def fetch(group):
        rows = pl.ds(group * GROUP * GRID, GROUP * GRID)
        planes = pl.ds(group * GROUP * 2 * GRID, GROUP * 2 * GRID)
        return (
            pltpu.make_async_copy(tiles_hbm.at[rows], tiles.at[rows], load_sems.at[0, group]),
            pltpu.make_async_copy(region_hbm.at[planes], region.at[planes], load_sems.at[1, group]),
        )

    tables = copies_of(
        (lanes_hbm, rows_hbm, columns_hbm, symbol_hbm), (lanes_q, rows_q, columns_q, symbol), table_sems
    )
    for copy in fetch(0):
        copy.start()
    for copy in tables[:2]:
        copy.start()
    for group in range(1, GROUPS):
        for copy in fetch(group):
            copy.start()
    for copy in tables[2:]:
        copy.start()
    for copy in tables[:2]:
        copy.wait()

    def put(buffer, target, pair, sem):
        for plane in (2 * pair, 2 * pair + 1):
            pltpu.make_async_copy(
                buffer.at[block_of(plane), :],
                target.at[0, :, pl.ds(pl.multiple_of(plane * 128, 128), 128)],
                sem,
            ).start()

    def head(group):
        for copy in fetch(group):
            copy.wait()
        values = []
        for pair in pairs_of(group):
            value = unfold_pair(tiles[block_of(pair), :]) * both_planes(region, pair, block_of)
            put_both_planes(gradient, pair, value, block_of)
            put(gradient, gradient_out, pair, sems.at[1])
            values.append(value)
        turned = unstacked(along_lanes(lanes_q[...], stacked(values)))
        for pair, value in zip(pairs_of(group), turned):
            put_both_planes(work, pair, along_rows(rows_q[...], value))

    loop(GROUPS, head, GROUPS)
    for copy in tables[2:]:
        copy.wait()

    def middle(step):
        first = 4 * step
        modes = along_rows(columns_q[...], columns_of(work, first)) * symbol[block_of(step), :]
        put_columns(work, first, along_rows(columns_q[...], modes))

    loop(GRID // 4, middle, MIDDLE_UNROLL)
    wait_planes(gradient, sems.at[1])

    def tail(group):
        values = [along_rows(rows_q[...], both_planes(work, pair)) for pair in pairs_of(group)]
        turned = unstacked(along_lanes(lanes_q[...], stacked(values)))
        for pair, value in zip(pairs_of(group), turned):
            put_both_planes(gradient, pair, value * both_planes(region, pair, block_of), block_of)
            put(gradient, preconditioned_out, pair, sems.at[2])

    loop(GROUPS, tail, GROUPS)
    wait_planes(gradient, sems.at[2])


MIDDLE_UNROLL = GRID // 4


def in_vmem(count):
    return [pl.BlockSpec(memory_space=pltpu.VMEM)] * count


def anywhere(count):
    return [pl.BlockSpec(memory_space=pl.ANY)] * count


FIELD = (GRID * PLANES, 128)
TILES = (8 * DEVICES, 128)


def precondition(tiles, region):
    modes = hartley()
    field = pltpu.VMEM(FIELD, F32)
    pitched = pltpu.VMEM(PITCHED, F32)
    shape = jax.ShapeDtypeStruct((1, GRID, GRID * GRID), F32)
    tables = [
        jnp.asarray(table)
        for table in (lanes_table(modes), rows_table(modes), columns_table(modes), chebyshev_symbol())
    ]
    return pl.pallas_call(
        precondition_kernel,
        out_shape=(shape, shape),
        in_specs=anywhere(2 + len(tables)),
        out_specs=anywhere(2),
        scratch_shapes=[pltpu.VMEM(table.shape, table.dtype) for table in tables] + [
            pltpu.VMEM(TILES, F32), field, field, pitched,
            pltpu.SemaphoreType.DMA((len(tables),)),
            pltpu.SemaphoreType.DMA((2, GROUPS)),
            pltpu.SemaphoreType.DMA((3,)),
        ],
        compiler_params=pltpu.CompilerParams(vmem_limit_bytes=VMEM_LIMIT),
        name="precondition",
    )(tiles, region, *tables)


def hamiltonian_tables():
    kinetic = -KINETIC_SCALE * circulant(kinetic_taps(), -14, GRID)
    magic = circulant(magic_taps(), -7, GRID)
    tables = (
        lanes_table_of_two(kinetic, magic),
        rows_table(kinetic),
        rows_table(magic),
        columns_table(kinetic),
        columns_table(magic),
        columns_table(magic.T),
        rows_table(magic.T),
        lanes_table(magic.T),
    )
    return [jnp.asarray(table) for table in tables]


def tile_of(index):
    return pl.ds(pl.multiple_of(index * BLOCK, BLOCK), BLOCK)


def spaced(index):
    return pl.ds(index * SPACE, BLOCK)


def row_of(index):
    return pl.ds(index, 1)


TEAMS = 4
CHIPS = DEVICES // 2
TEAM = CHIPS // TEAMS
BLOCK = 16
SPACE = BLOCK + 1
LOGICAL = pl.DeviceIdType.LOGICAL
SEND_UNROLL = 8
EARLY = 2


def gradient_kernel(
    wave, potential_hbm,
    runs_hbm, kf_hbm, k_hbm, f_hbm, ck_hbm, cf_hbm, cb_hbm, b_hbm, lb_hbm,
    gradient_tiles, region_out,
    runs, lanes_kf, rows_k, rows_f, columns_k, columns_f, columns_b, rows_b, lanes_b,
    waves, staged, region, masked, kinetic, forward, potential,
    masked_send, masked_recv, applied_send, applied_recv, back_send,
    masked_split, partial, gathered, row, matrix,
    table_sems, load_sems, send_sems, recv_sems,
):
    chip = lax.axis_index("orb")
    core = lax.axis_index("pair")
    device = chip * 2 + core
    my_team = jnp.bitwise_and(lax.shift_right_logical(chip, 1), 2) + jnp.bitwise_and(chip, 1)
    my_seat = jnp.bitwise_and(lax.shift_right_logical(chip, 2), 14) + jnp.bitwise_and(
        lax.shift_right_logical(chip, 1), 1
    )
    me = my_team * TEAM + my_seat
    my_half = core * CHIPS
    barrier = pltpu.get_barrier_semaphore()

    def greet(step):
        peer = jnp.bitwise_xor(device, 2 * (CHIPS - 1 - step))
        pl.semaphore_signal(barrier, inc=1, device_id=peer, device_id_type=LOGICAL)

    tables = copies_of(
        (runs_hbm, kf_hbm, k_hbm, f_hbm, ck_hbm, cf_hbm, cb_hbm, b_hbm, lb_hbm),
        (runs, lanes_kf, rows_k, rows_f, columns_k, columns_f, columns_b, rows_b, lanes_b),
        table_sems,
    )
    tables[0].start()
    load_planes(wave.at[0], waves, load_sems.at[0])
    for copy in tables[1:]:
        copy.start()
    loop(CHIPS - 1, greet, SEND_UNROLL)
    partner = jnp.bitwise_xor(device, 1)
    pl.semaphore_signal(barrier, inc=1, device_id=partner, device_id_type=LOGICAL)
    load_planes(potential_hbm, staged, load_sems.at[1])
    tables[0].wait()
    bounds = run_bounds(runs[...])
    wait_planes(waves, load_sems.at[0])

    def team_at(stage):
        return jnp.bitwise_xor(my_team, stage)

    def send_team(source, target, phase, stage, source_at, target_at, signal):
        apart = (stage & 2) * 4 + (stage & 1) * 2

        def send(step):
            seat = TEAM - 1 - step
            pltpu.make_async_remote_copy(
                src_ref=source.at[source_at(jnp.bitwise_xor(me, stage * TEAM + seat))],
                dst_ref=target.at[target_at(me)],
                send_sem=send_sems.at[phase],
                recv_sem=recv_sems.at[phase, signal],
                device_id=jnp.bitwise_xor(
                    device, jnp.bitwise_and(seat, 14) * 8 + jnp.bitwise_and(seat, 1) * 4 + apart
                ),
                device_id_type=LOGICAL,
            ).start()

        loop(size_of(stage), send, size_of(stage))

    def size_of(stage):
        return TEAM if stage else TEAM - 1

    def scatter(source, target, phase, source_at, target_at, signal=0):
        for stage in range(TEAMS):
            send_team(source, target, phase, stage, source_at, target_at, signal)

    def drain(buffer, sem, count=CHIPS - 1):
        whole = buffer.at[pl.ds(0, buffer.shape[0] * count // CHIPS)]
        pltpu.make_async_copy(whole, whole, sem).wait()

    def mask_pair(pair):
        mask = region_pair(bounds, pair)
        put_both_planes(region, pair, mask, block_of)
        value = both_planes(waves, pair, block_of) * mask
        put_both_planes(masked, pair, value)
        masked_send[block_of(pair), :] = fold_pair(value)

    def head(group):
        values = [both_planes(masked, pair) for pair in pairs_of(group)]
        hamiltonian_head(kinetic, forward, (lanes_kf, rows_k, rows_f), group, values)

    loop(PLANES // 2, mask_pair, PLANES // 2)
    region_copy = pltpu.make_async_copy(region, region_out, load_sems.at[2])
    region_copy.start()
    for copy in tables[1:]:
        copy.wait()
    for group in range(EARLY):
        head(group)
    pl.semaphore_wait(barrier, CHIPS)
    scatter(masked_send, masked_recv, 0, tile_of, lambda label: spaced(my_half + label))
    masked_recv[spaced(my_half + me), :] = masked_send[tile_of(me), :]
    for group in range(EARLY, GROUPS):
        head(group)
    wait_planes(staged, load_sems.at[1])

    def pitch(pair):
        put_both_planes(potential, pair, both_planes(staged, pair, block_of))

    loop(PLANES // 2, pitch, 4)

    def middle(step):
        hamiltonian_middle(
            masked, kinetic, forward, potential, (columns_k, columns_f, columns_b), step
        )

    loop(GRID // 4, middle, MIDDLE_UNROLL)

    def tail(stage):
        team = team_at(stage)
        values = hamiltonian_tail(kinetic, forward, (rows_b, lanes_b), team)
        for pair, value in zip(pairs_of(team), values):
            applied_send[block_of(pair), :] = fold_pair(value * both_planes(region, pair, block_of))
        send_team(applied_send, applied_recv, 1, stage, tile_of, spaced, my_team)

    for stage in range(TEAMS):
        tail(stage)
    applied_recv[spaced(me), :] = applied_send[tile_of(me), :]
    drain(masked_send, recv_sems.at[0, 0])
    kind = masked_recv.at[pl.ds(pl.multiple_of(my_half * SPACE, 8), CHIPS * SPACE), :]
    swap = pltpu.make_async_remote_copy(
        src_ref=kind, dst_ref=kind, send_sem=send_sems.at[5], recv_sem=recv_sems.at[5, 0],
        device_id=partner, device_id_type=LOGICAL,
    )
    swap.start()

    def split_half(first):
        for sub in range(BLOCK):
            rows = pl.ds(first * SPACE + sub, CHIPS, stride=SPACE)
            high, low = split_pair(masked_recv[rows, :])
            lanes = slice(sub * 128, sub * 128 + 128)
            masked_split[pl.ds(pl.multiple_of(first, CHIPS), CHIPS), lanes] = high
            masked_split[pl.ds(pl.multiple_of(first, CHIPS) + DEVICES, CHIPS), lanes] = low

    split_half(my_half)
    swap.wait()
    split_half(CHIPS - my_half)

    def strided(team, sub):
        return pl.ds(team * (TEAM * SPACE) + sub, TEAM, stride=SPACE)

    def correlate(stage):
        team = team_at(stage)
        drain(applied_send, recv_sems.at[1, team], size_of(stage))
        parts = [split_pair(applied_recv[strided(team, sub), :]) for sub in range(BLOCK)]
        left = jnp.concatenate(
            [jnp.concatenate([part[which] for part in parts], axis=1) for which in range(2)], axis=0
        )
        total = lax.dot_general(
            left, masked_split[...], (((1,), (1,)), ((), ())), preferred_element_type=F32
        )
        rows = total[:TEAM, :DEVICES] + (total[:TEAM, DEVICES:] + total[TEAM:, :DEVICES])
        partial[pl.ds(team * TEAM, TEAM), 0, :] = rows
        send_team(partial, gathered, 2, stage, row_of, row_of, 0)

    for stage in range(TEAMS):
        correlate(stage)
    gathered[row_of(me)] = partial[row_of(me)]
    drain(gathered, recv_sems.at[2, 0])
    row[...] = jnp.sum(gathered[...], axis=0, keepdims=True) * (1.0 / CELLS)
    scatter(row, matrix, 3, lambda peer: pl.ds(0, 1), row_of, my_team)
    matrix[row_of(me)] = row[...]

    def project(stage):
        team = team_at(stage)
        drain(matrix, recv_sems.at[3, team], size_of(stage))
        high, low = split_pair(matrix[pl.ds(team * TEAM, TEAM), 0, :])
        table = jnp.concatenate([high, high, low], axis=1)
        for sub in range(0, BLOCK, 2):
            lanes = slice(sub * 128, sub * 128 + 256)
            projected = dot32(
                table,
                jnp.concatenate([masked_split[:, lanes], masked_split[:DEVICES, lanes]], axis=0),
            )
            for shift in range(2):
                rows = strided(team, sub + shift)
                back_send[rows, :] = (
                    applied_recv[rows, :] - projected[:, shift * 128 : shift * 128 + 128]
                )
        send_team(back_send, gradient_tiles, 4, stage, spaced, tile_of, 0)

    for stage in range(TEAMS):
        project(stage)
    own = pltpu.make_async_copy(back_send.at[spaced(me)], gradient_tiles.at[tile_of(me)], load_sems.at[3])
    own.start()
    region_copy.wait()
    own.wait()
    drain(masked_send, send_sems.at[0])
    drain(applied_send, send_sems.at[1])
    drain(partial, send_sems.at[2])
    drain(matrix, send_sems.at[3])
    drain(gradient_tiles, recv_sems.at[4, 0])
    drain(gradient_tiles, send_sems.at[4])


def gradient_fields(wavefunctions, potential, line_runs):
    field = pltpu.VMEM(FIELD, F32)
    pitched = pltpu.VMEM(PITCHED, F32)
    tiles = pltpu.VMEM(TILES, F32)
    spaces = pltpu.VMEM((CHIPS * SPACE, 128), F32)
    rows = pltpu.VMEM((CHIPS, 1, 128), F32)
    tables = [line_runs, *hamiltonian_tables()]
    return pl.pallas_call(
        gradient_kernel,
        out_shape=(jax.ShapeDtypeStruct(TILES, F32), jax.ShapeDtypeStruct(FIELD, F32)),
        in_specs=anywhere(2 + len(tables)),
        out_specs=anywhere(2),
        scratch_shapes=[pltpu.VMEM(table.shape, table.dtype) for table in tables] + [
            field, field, field, pitched, pitched, pitched, pitched,
            tiles, pltpu.VMEM((DEVICES * SPACE, 128), F32), tiles, spaces, spaces,
            pltpu.VMEM((2 * DEVICES, BLOCK * 128), BF16),
            rows, rows, pltpu.VMEM((1, 1, 128), F32), rows,
            pltpu.SemaphoreType.DMA((len(tables),)),
            pltpu.SemaphoreType.DMA((4,)),
            pltpu.SemaphoreType.DMA((6,)),
            pltpu.SemaphoreType.DMA((6, TEAMS)),
        ],
        compiler_params=pltpu.CompilerParams(
            collective_id=0, has_side_effects=True, vmem_limit_bytes=VMEM_LIMIT
        ),
        name="gradient",
    )(wavefunctions, potential, *tables)


def on_device(wavefunctions, potential, line_runs):
    tiles, region = gradient_fields(wavefunctions, potential, line_runs)
    return precondition(tiles, region)


def solution(mesh):
    return jax.shard_map(
        on_device,
        mesh=mesh,
        in_specs=(P(("orb", "pair"), None, None), P(), P()),
        out_specs=(P(("orb", "pair"), None, None), P(("orb", "pair"), None, None)),
        check_vma=False,
    )
```
